256 devices in a mesh: depth: 16 (over x, y), view: 16 (over z, core).
Axes of the slice: x: 4, y: 4, z: 8, core: 2. Of those that a mesh axis runs over, the one named last changes fastest.
Arguments:
- bricks: float32 [16, 16, 8, 64, 4096], P('depth', 'view'), may hold values from -6 to 6
- tile_holder: int32 [16, 16, 8], P('depth', 'view'), may hold values from -1 to 15, as said below
Outputs:
- image: float32 [4, 64, 8192], P(None, 'depth', 'view')
The draws below stay inside these ranges and needn't reach their ends.
Inputs may be any that keep to these rules, and one draw needn't show every extreme that they name: Renderer (d, v) finds brick column t in slot t of holder tile_holder[d, v, t]. For fixed d and t the holders that appear are distinct over v, and the holders named by one renderer are distinct; brick column 0 is never skipped.
All inputs are finite; a program needn't handle non-finite values.
Results may differ from the reference program's by a relative error of at most 0.0003.
Values sent between devices are 32-bit elements; how exact they have to be, the bound alone decides.
A program may use at most 128 MiB of HBM per device.

```python
import jax
import jax.numpy as jnp
from jax import lax

BS = 64
TC_DEV = 8
STEPS = 48
N_DEPTH = 16
N_VIEW = 16


def draw_tile_holder(key, part):
    keys = jax.random.split(jax.random.fold_in(key, 17), 5)
    shuffle_keys = jax.random.split(keys[0], N_DEPTH)
    holder_perm = jax.vmap(lambda item: jax.random.permutation(item, N_VIEW))(shuffle_keys)
    shift_keys = jax.random.split(keys[1], N_DEPTH)
    shifts = jax.vmap(lambda item: jax.random.permutation(item, N_VIEW)[:TC_DEV])(shift_keys)
    views = jnp.arange(N_VIEW, dtype=jnp.int32)
    spots = (views[None, :, None] + shifts[:, None, :]) % N_VIEW
    holders = jax.vmap(lambda perm, where_at: perm[where_at])(holder_perm, spots)
    counts = jax.random.randint(keys[2], (N_DEPTH, N_VIEW), 1, TC_DEV + 1)
    lowest = jax.random.randint(keys[3], (N_DEPTH,), 0, N_VIEW)
    counts = jnp.where(views[None, :] == lowest[:, None], 1, counts)
    rank_keys = jax.random.split(keys[4], N_DEPTH * N_VIEW)
    ranks = jax.vmap(lambda item: jax.random.permutation(item, TC_DEV - 1))(rank_keys).reshape(N_DEPTH, N_VIEW, TC_DEV - 1)
    drawn_rest = ranks < counts[:, :, None] - 1
    drawn = jnp.concatenate([jnp.ones((N_DEPTH, N_VIEW, 1), dtype=bool), drawn_rest], axis=2)
    return jnp.where(drawn, holders, -1).astype(jnp.int32)


def steps_of(own_key, extent, cuts, smallest, largest):
    def one(position, blocks):
        steps = jax.random.uniform(jax.random.fold_in(jax.random.fold_in(own_key, 6), position), (blocks,), jnp.float32, smallest / len(cuts), largest / len(cuts))
        return jnp.repeat(jnp.exp(steps), extent[position] // blocks).reshape((-1,) + (1,) * (len(extent) - position - 1))

    level = one(*cuts[0])
    for cut in cuts[1:]:
        level = level * one(*cut)
    return level


def centred(stream_key, extent, spread, reach, cuts=(), kind=jnp.bfloat16):
    entries = jax.random.normal(stream_key, extent, jnp.float32) * spread
    if len(cuts) > 0:
        entries = steps_of(stream_key, extent, cuts, -0.22, 0.18) * entries
    return jnp.clip(entries, min=-reach, max=reach).astype(kind)


def setup_inputs(seed: int = 0) -> dict:
    arg_keys = jax.random.split(jax.random.key(seed), 3)
    bricks = centred(arg_keys[0], (N_DEPTH, N_VIEW, TC_DEV, BS, BS * BS), 1.0, 6.0, ((0, 16), (1, 16)), jnp.float32)
    tile_holder = draw_tile_holder(jax.random.fold_in(arg_keys[2], 71), 0)
    return dict(bricks=bricks, tile_holder=tile_holder)


DENSITY = 0.8
ISO_LEVEL = 1.0
SHARPEN = 1.5

def sample_table():
    spots = (jnp.arange(STEPS, dtype=jnp.float32) + 0.5) * (BS / STEPS) - 0.5
    spots = jnp.clip(spots, 0.0, BS - 1.0)
    voxels = jnp.arange(BS, dtype=jnp.float32)
    return jnp.maximum(0.0, 1.0 - jnp.abs(spots[:, None] - voxels[None, :])).astype(jnp.float32)

def prefix_table():
    steps_idx = jnp.arange(STEPS, dtype=jnp.int32)
    return (steps_idx[:, None] > steps_idx[None, :]).astype(jnp.float32)

def neighbor_diff(values):
    flat_idx = jnp.arange(BS * BS, dtype=jnp.int32)
    column = flat_idx % BS
    rowpos = flat_idx // BS
    right = jnp.where(column == BS - 1, values, jnp.roll(values, -1, axis=1))
    left = jnp.where(column == 0, values, jnp.roll(values, 1, axis=1))
    below = jnp.where(rowpos == BS - 1, values, jnp.roll(values, -BS, axis=1))
    above = jnp.where(rowpos == 0, values, jnp.roll(values, BS, axis=1))
    ahead = jnp.concatenate([values[1:], values[-1:]], axis=0)
    behind = jnp.concatenate([values[:1], values[:-1]], axis=0)
    return (right - left, below - above, ahead - behind)

def march_brick(brick, table, prefix):
    samples = jnp.dot(table, brick, precision=lax.Precision.HIGHEST)
    grad_x, grad_y, grad_z = neighbor_diff(samples)
    shade = 0.3 + 0.7 * jnp.abs(grad_z) / jnp.sqrt(grad_x * grad_x + grad_y * grad_y + grad_z * grad_z + 1.0)
    thickness = DENSITY / STEPS * jax.nn.sigmoid(4.0 * (samples - ISO_LEVEL))
    optical = jnp.dot(prefix, thickness, precision=lax.Precision.HIGHEST)
    weight = jnp.exp(-optical) * (1.0 - jnp.exp(-thickness))
    lit = weight * shade
    red_sum = lax.optimization_barrier(jnp.sum(lit * jax.nn.sigmoid(1.5 * samples), axis=0))
    green_sum = lax.optimization_barrier(jnp.sum(lit * jax.nn.sigmoid(-1.5 * samples), axis=0))
    blue_sum = lax.optimization_barrier(jnp.sum(lit * jax.nn.sigmoid(3.0 * (samples - 1.0)), axis=0))
    opacity = lax.optimization_barrier(jnp.sum(weight, axis=0))
    return jnp.stack([red_sum, green_sum, blue_sum, opacity], axis=0)

def composite_over(front, back, axis):
    front_alpha = lax.slice_in_dim(front, 3, 4, axis=axis)
    return front + (1.0 - front_alpha) * back

def sharpen_image(composite):
    padded = jnp.pad(composite, ((0, 0), (1, 1), (1, 1)))
    rows_done = 0.25 * padded[:, :-2] + 0.5 * padded[:, 1:-1] + 0.25 * padded[:, 2:]
    blurred = 0.25 * rows_done[:, :, :-2] + 0.5 * rows_done[:, :, 1:-1] + 0.25 * rows_done[:, :, 2:]
    return composite + SHARPEN * (composite - blurred)

def reference(bricks, tile_holder):
    table = sample_table()
    prefix = prefix_table()

    def render_slab(inputs):
        stored, holders = inputs
        flat = stored.reshape(N_VIEW * TC_DEV, BS, BS * BS)
        columns = jnp.arange(TC_DEV, dtype=jnp.int32)[None, :]
        indices = (jnp.clip(holders, 0, N_VIEW - 1) * TC_DEV + columns).reshape(-1).astype(jnp.int32)
        visible = (holders >= 0).astype(jnp.float32).reshape(-1)

        def one_tile(pair):
            index_one, shown = pair
            return march_brick(flat[index_one], table, prefix) * shown
        tiles = lax.map(one_tile, (indices, visible))
        tiles = tiles.reshape(N_VIEW * TC_DEV, 4, BS, BS)
        return tiles.transpose(1, 2, 0, 3).reshape(4, BS, N_VIEW * TC_DEV * BS)
    current = lax.map(render_slab, (bricks, tile_holder))
    while current.shape[0] > 1:
        paired = current.reshape((current.shape[0] // 2, 2) + current.shape[1:])
        current = composite_over(paired[:, 0], paired[:, 1], 1)
    return sharpen_image(current[0])
```

```python
import math

import jax
import jax.numpy as jnp
from jax import lax
from jax.experimental import pallas as pl
from jax.experimental.pallas import tpu as pltpu
from jax.sharding import PartitionSpec as P

STEPS = 48
DENSITY = 0.8
SHARPEN = 1.5
PERIODS = 16
UNROLL = 4
HALF = DENSITY / STEPS / 2.0
LOG2E = math.log2(math.e)


def render_slot(load, store):
    shape = (8, 128)
    lane = lax.broadcasted_iota(jnp.int32, shape, 1)
    row = lax.broadcasted_iota(jnp.int32, shape, 0)
    x = lax.rem(lane, 64)
    first_x = x == 0
    last_x = x == 63
    low = lane < 64
    top = row == 0
    bottom = row == 7

    def plane_terms(cur):
        out = []
        swapped = [pltpu.roll(c, 64, 1) for c in cur]
        before0 = jnp.where(top, cur[0], pltpu.roll(swapped[3], 1, 0))
        delta = [swapped[0] - before0]
        for g in range(1, 4):
            delta.append(swapped[g] - swapped[g - 1])
        delta.append(jnp.where(bottom, cur[3] - swapped[3], pltpu.roll(delta[0], 7, 0)))
        for g in range(4):
            c = cur[g]
            right = jnp.where(last_x, c, pltpu.roll(c, 127, 1))
            left = jnp.where(first_x, c, pltpu.roll(c, 1, 1))
            gx = right - left
            gy = jnp.where(low, delta[g], delta[g + 1])
            out.append(gx * gx + gy * gy + 36.0)
        return out

    def shade_step(state, cur, plane, behind, ahead):
        trans, acc_a, acc_b, acc_c = state
        new = ([], [], [], [])
        for g in range(4):
            c = cur[g]
            gz = ahead[g] - behind[g]
            slope = jnp.abs(gz) * lax.rsqrt(plane[g] + gz * gz)
            dense = jnp.tanh(c * (1.0 / 3.0) - 2.0)
            kept = jnp.exp2(dense * (-LOG2E * HALF) + (-LOG2E * HALF))
            after = trans[g] * kept
            lit = (trans[g] - after) * (slope + (3.0 / 7.0))
            new[0].append(after)
            new[1].append(acc_a[g] + lit)
            new[2].append(acc_b[g] + lit * jnp.tanh(c * 0.125))
            new[3].append(acc_c[g] + lit * jnp.tanh(c * 0.25 - 1.5))
        return new

    def period_samples(k):
        three = ([], [], [])
        for g in range(4):
            b0, b1, b2, b3 = (load(4 * k + j, g) for j in range(4))
            three[0].append(5.0 * b0 + b1)
            three[1].append(3.0 * (b1 + b2))
            three[2].append(b2 + 5.0 * b3)
        return three

    zeros = [jnp.zeros(shape, jnp.float32)] * 4
    ones = [jnp.ones(shape, jnp.float32)] * 4
    state = (ones, zeros, zeros, zeros)
    p0, p1, p2 = period_samples(0)
    state = shade_step(state, p0, plane_terms(p0), p0, p1)
    state = shade_step(state, p1, plane_terms(p1), p0, p2)
    carry = (p1, p2, plane_terms(p2), state)

    def one_period(k, carry):
        behind, last, last_plane, state = carry
        a, b, c = period_samples(k)
        state = shade_step(state, last, last_plane, behind, a)
        state = shade_step(state, a, plane_terms(a), last, b)
        state = shade_step(state, b, plane_terms(b), a, c)
        return (b, c, plane_terms(c), state)

    carry = lax.fori_loop(1, PERIODS, one_period, carry, unroll=True)
    behind, last, last_plane, state = carry
    trans, acc_a, acc_b, acc_c = shade_step(state, last, last_plane, behind, last)
    for g in range(4):
        store(0, g, 0.35 * (acc_a[g] + acc_b[g]))
        store(1, g, 0.35 * (acc_a[g] - acc_b[g]))
        store(2, g, 0.35 * (acc_a[g] + acc_c[g]))
        store(3, g, 1.0 - trans[g])


def render_kernel(bricks_ref, out_ref):
    def load(z, g):
        return bricks_ref[0, z // 8, pl.ds(g * 8 + z % 8, 8, stride=32), :]

    def store(ch, g, value):
        out_ref[0, pl.ds((g // 2) * 8 + ch * 2 + g % 2, 8, stride=16), :] = value

    render_slot(load, store)


def render(bricks):
    slots = bricks.shape[0]
    return pl.pallas_call(
        render_kernel,
        grid=(slots,),
        in_specs=[pl.BlockSpec((1, 8, 256, 128), lambda t: (t, 0, 0, 0))],
        out_specs=pl.BlockSpec((1, 128, 128), lambda t: (t, 0, 0)),
        out_shape=jax.ShapeDtypeStruct((slots, 128, 128), jnp.float32),
        name="render",
    )(bricks)


def as_tiles(stored):
    slots, edge, pixels = stored.shape
    split = stored.reshape(slots, edge // 8, 8, pixels // 128, 128)
    return split.transpose(0, 1, 3, 2, 4).reshape(slots, edge // 8, pixels // 16, 128)


def padded_2(x, sides, width):
    for axis, dim in sides:
        size, length = (lax.axis_size(axis), x.shape[dim])
        up = [(i, (i + 1) % size) for i in range(size - 1)]
        down = [(j, i) for i, j in up]
        last = lax.slice_in_dim(x, length - width, length, axis=dim)
        initial = lax.slice_in_dim(x, 0, width, axis=dim)
        before = lax.ppermute(last, axis, up)
        after = lax.ppermute(initial, axis, down)
        x = jnp.concatenate([before, x, after], axis=dim)
    return x


def body(bricks, tile_holder):
    me = lax.axis_index("view")
    tiles = render(as_tiles(bricks[0, 0]))
    table = lax.all_gather(tile_holder[0, 0], "view")
    table = lax.all_gather(table, "depth")
    slot_ids = jnp.arange(8, dtype=jnp.int32)
    slot = jnp.max(jnp.where(table == me, slot_ids, 0), axis=2)
    bands = tiles.reshape(8, 16, 8, 128).transpose(1, 0, 2, 3)
    held = lax.all_to_all(bands, "depth", split_axis=0, concat_axis=0, tiled=True)
    flat = held.reshape(16 * 8, 8, 128)
    index = (jnp.arange(16, dtype=jnp.int32)[None, :] * 8 + slot.T).reshape(-1)
    outgoing = flat[index].reshape(16, 16, 8, 128)
    arrived = lax.all_to_all(outgoing, "view", split_axis=0, concat_axis=0, tiled=True)
    mine = lax.dynamic_index_in_dim(table, me, 1, keepdims=False)
    where_at = jnp.maximum(mine, 0) * 16 + jnp.arange(16, dtype=jnp.int32)[:, None]
    pieces = arrived.reshape(256, 8, 128)[where_at.reshape(-1)].reshape(16, 8, 4, 2, 128)
    pieces = pieces * (mine >= 0).astype(jnp.float32)[:, :, None, None, None]
    current = pieces
    while current.shape[0] > 1:
        pair = current.reshape((current.shape[0] // 2, 2) + current.shape[1:])
        current = pair[:, 0] + (1.0 - pair[:, 0, :, 3:4]) * pair[:, 1]
    merged = current[0]
    block = merged.reshape(8, 4, 4, 64).transpose(1, 2, 0, 3).reshape(4, 4, 512)
    padded = padded_2(block, (("depth", 1), ("view", 2)), 1)
    rows_done = 0.25 * padded[:, :-2] + 0.5 * padded[:, 1:-1] + 0.25 * padded[:, 2:]
    blurred = 0.25 * rows_done[:, :, :-2] + 0.5 * rows_done[:, :, 1:-1] + 0.25 * rows_done[:, :, 2:]
    return block + SHARPEN * (block - blurred)


def solution(mesh):
    in_specs = (P("depth", "view", None, None, None), P("depth", "view", None))
    out_specs = P(None, "depth", "view")
    return jax.shard_map(body, mesh=mesh, in_specs=in_specs, out_specs=out_specs, check_vma=False)
```

```python
import math

import jax
import jax.numpy as jnp
from jax import lax
from jax.experimental import pallas as pl
from jax.experimental.pallas import tpu as pltpu
from jax.sharding import PartitionSpec as P

STEPS = 48
DENSITY = 0.8
SHARPEN = 1.5
PERIODS = 16
UNROLL = 4
HALF = DENSITY / STEPS / 2.0
LOG2E = math.log2(math.e)


def render_slot(load, store):
    shape = (8, 128)
    lane = lax.broadcasted_iota(jnp.int32, shape, 1)
    row = lax.broadcasted_iota(jnp.int32, shape, 0)
    x = lax.rem(lane, 64)
    first_x = x == 0
    last_x = x == 63
    low = lane < 64
    top = row == 0
    bottom = row == 7

    def plane_terms(cur):
        before = jnp.where(top, pltpu.roll(cur[0], 64, 1), pltpu.roll(cur[3], 1, 0))
        after = jnp.where(bottom, pltpu.roll(cur[3], 64, 1), pltpu.roll(cur[0], 7, 0))
        line = [before] + cur + [after]
        step = [line[i + 1] - line[i] for i in range(5)]
        out = []
        for g in range(4):
            c = cur[g]
            right = jnp.where(last_x, c, pltpu.roll(c, 127, 1))
            left = jnp.where(first_x, c, pltpu.roll(c, 1, 1))
            gx = right - left
            gy = pltpu.roll(jnp.where(low, step[g + 1], step[g]), 64, 1)
            out.append(gx * gx + gy * gy + 36.0)
        return out

    def shade_step(state, cur, plane, behind, ahead):
        trans, acc_a, acc_b, acc_c = state
        new = ([], [], [], [])
        for g in range(4):
            c = cur[g]
            gz = ahead[g] - behind[g]
            slope = jnp.abs(gz) * lax.rsqrt(plane[g] + gz * gz)
            dense = jnp.tanh(c * (1.0 / 3.0) - 2.0)
            kept = jnp.exp2(dense * (-LOG2E * HALF) + (-LOG2E * HALF))
            after = trans[g] * kept
            lit = (trans[g] - after) * (slope + (3.0 / 7.0))
            new[0].append(after)
            new[1].append(acc_a[g] + lit)
            new[2].append(acc_b[g] + lit * jnp.tanh(c * 0.125))
            new[3].append(acc_c[g] + lit * jnp.tanh(c * 0.25 - 1.5))
        return new

    def period_samples(k):
        three = ([], [], [])
        for g in range(4):
            b0, b1, b2, b3 = (load(4 * k + j, g) for j in range(4))
            three[0].append(5.0 * b0 + b1)
            three[1].append(3.0 * (b1 + b2))
            three[2].append(b2 + 5.0 * b3)
        return three

    zeros = [jnp.zeros(shape, jnp.float32)] * 4
    ones = [jnp.ones(shape, jnp.float32)] * 4
    state = (ones, zeros, zeros, zeros)
    p0, p1, p2 = period_samples(0)
    state = shade_step(state, p0, plane_terms(p0), p0, p1)
    state = shade_step(state, p1, plane_terms(p1), p0, p2)
    carry = (p1, p2, plane_terms(p2), state)

    def one_period(k, carry):
        behind, last, last_plane, state = carry
        a, b, c = period_samples(k)
        state = shade_step(state, last, last_plane, behind, a)
        state = shade_step(state, a, plane_terms(a), last, b)
        state = shade_step(state, b, plane_terms(b), a, c)
        return (b, c, plane_terms(c), state)

    carry = lax.fori_loop(1, PERIODS, one_period, carry, unroll=True)
    behind, last, last_plane, state = carry
    trans, acc_a, acc_b, acc_c = shade_step(state, last, last_plane, behind, last)
    for g in range(4):
        store(0, g, 0.35 * (acc_a[g] + acc_b[g]))
        store(1, g, 0.35 * (acc_a[g] - acc_b[g]))
        store(2, g, 0.35 * (acc_a[g] + acc_c[g]))
        store(3, g, 1.0 - trans[g])


def as_tiles(stored):
    slots, edge, pixels = stored.shape
    split = stored.reshape(slots, edge // 8, 8, pixels // 128, 128)
    return split.transpose(0, 1, 3, 2, 4).reshape(slots, edge // 8, pixels // 16, 128)


N = 16
SLOTS = 8
GROUP = 2
GROUPS = SLOTS // GROUP
CAP = 16
MESH = pl.DeviceIdType.MESH
SIDES = [(dd, dv) for dd in (-1, 0, 1) for dv in (-1, 0, 1) if (dd, dv) != (0, 0)]


def wrap(i):
    return lax.rem(i + N, N)


def fused_kernel(
    holders, bricks, image, most, buf, dsend, held, zsend, zrecv, comp, row_in, slab, table,
    vidx, vpos, sidx, spos, front, edges, above, below, from_left, from_right, side,
    brick_sem, row_send, row_recv, slab_send, slab_recv, local_sem,
    d_send, d_recv, z_send, z_recv, rim_send, rim_recv,
):
    dm = lax.axis_index("depth")
    vm = lax.axis_index("view")
    lane8 = lax.broadcasted_iota(jnp.int32, (8, 128), 1)
    sub8 = lax.broadcasted_iota(jnp.int32, (8, 128), 0)
    lane16 = lax.broadcasted_iota(jnp.int32, (N, 128), 1)
    sub16 = lax.broadcasted_iota(jnp.int32, (N, 128), 0)

    def remote(src, dst, send, recv, target):
        return pltpu.make_async_remote_copy(
            src_ref=src, dst_ref=dst, send_sem=send, recv_sem=recv,
            device_id=target, device_id_type=MESH,
        )

    def others(step):
        def run(i, carry):
            step(i)
            return carry
        lax.fori_loop(1, N, run, 0)

    barrier = pltpu.get_barrier_semaphore()

    def greet(i):
        pl.semaphore_signal(barrier, inc=1, device_id=(dm, wrap(vm + i)), device_id_type=MESH)
        pl.semaphore_signal(barrier, inc=1, device_id=(wrap(dm + i), vm), device_id_type=MESH)

    others(greet)
    for dd, dv in SIDES:
        if dd != 0 and dv != 0:
            target = (wrap(dm + dd), wrap(vm + dv))
            pl.semaphore_signal(barrier, inc=1, device_id=target, device_id_type=MESH)

    def brick_copy(t):
        return pltpu.make_async_copy(bricks.at[t], buf.at[t], brick_sem.at[t])

    for t in range(SLOTS):
        brick_copy(t).start()
    pl.semaphore_wait(barrier, 2 * (N - 1) + 4)

    mine = jnp.full((8, 128), -1, jnp.int32)
    for t in range(SLOTS):
        mine = jnp.where(lane8 == t, holders[t], mine)
    row_in[vm] = mine

    def row_copy(i, source):
        return remote(row_in.at[source], row_in.at[source], row_send.at[i], row_recv.at[source],
                      (dm, wrap(vm + i)))

    others(lambda i: row_copy(i, vm).start())

    def render_one(t):
        brick_copy(t).wait()

        def load(z, g):
            return buf[t, z // 8, pl.ds(g * 8 + z % 8, 8, stride=32), :]

        flat = dsend.reshape(N * SLOTS * 8, 128)

        def store(ch, g, value):
            first = ((g // 2) * SLOTS + t) * 8 + (g % 2) * 4 + ch
            flat[pl.ds(first, 8, stride=2 * SLOTS * 8), :] = value

        render_slot(load, store)

    def band_copy(k, i, source):
        target = wrap(dm + i)
        return remote(
            dsend.at[pl.ds(target * SLOTS + k * GROUP, GROUP)],
            held.at[pl.ds(source * SLOTS + k * GROUP, GROUP)],
            d_send.at[k, i], d_recv.at[k, source], (target, vm),
        )

    def slab_copy(i, source):
        return remote(slab, table.at[source], slab_send.at[i], slab_recv.at[source],
                      (wrap(dm + i), vm))

    def render_group(k, carry):
        def one(j, c):
            render_one(k * GROUP + j)
            return c

        lax.fori_loop(0, GROUP, one, 0)
        others(lambda i: band_copy(k, i, dm).start())
        for j in range(GROUP):
            held[dm * SLOTS + k * GROUP + j] = dsend[dm * SLOTS + k * GROUP + j]
        return carry

    lax.fori_loop(0, 1, render_group, 0)
    others(lambda i: row_copy(i, wrap(vm + i)).wait_recv())
    for v in range(N):
        slab[pl.ds(v, 1), :] = row_in[v, pl.ds(0, 1), :]
    table[dm] = slab[...]
    others(lambda i: slab_copy(i, dm).start())
    lax.fori_loop(1, GROUPS, render_group, 0)

    others(lambda i: slab_copy(i, wrap(dm + i)).wait_recv())
    listed = jnp.zeros((N, 128), jnp.int32)
    count = jnp.zeros((N, 128), jnp.int32)
    for d in range(N):
        slot = jnp.max(jnp.where(table[d] == vm, lane16, -1), axis=1, keepdims=True)
        wanted = slot >= 0
        listed = listed + jnp.where(wanted & (lane16 == count), slot + d * SLOTS, 0)
        count = count + jnp.where(wanted, 1, 0)
    vidx[...] = listed
    index_copy = pltpu.make_async_copy(vidx, sidx, local_sem.at[0])
    index_copy.start()
    index_copy.wait()

    def wait_bands(k, carry):
        others(lambda i: band_copy(k, i, wrap(dm + i)).wait_recv())
        return carry

    lax.fori_loop(0, GROUPS, wait_bands, 0)

    def tile_copy(i, source):
        target = wrap(vm + i)
        return remote(
            zsend.at[pl.ds(target * CAP, CAP)], zrecv.at[pl.ds(source * CAP, CAP)],
            z_send.at[i], z_recv.at[source], (dm, target),
        )

    def pack(i):
        target = wrap(vm + i)
        for j in range(CAP):
            zsend[target * CAP + j] = held[sidx[target, j]]
        tile_copy(i, vm).start()

    others(pack)
    for j in range(CAP):
        zrecv[vm * CAP + j] = held[sidx[vm, j]]

    count = jnp.zeros((N, 128), jnp.int32)
    for d in range(N):
        named = sub16 == table[d, pl.ds(vm, 1), :]
        place = jnp.where(named, sub16 * CAP + count + 1, 0)
        vpos[pl.ds(d, 1), :] = jnp.sum(place, axis=0, keepdims=True) - 1
        count = count + jnp.max(jnp.where(named, 1, 0), axis=1, keepdims=True)
    place_copy = pltpu.make_async_copy(vpos, spos, local_sem.at[1])
    place_copy.start()
    place_copy.wait()

    longest = jnp.zeros((N, 128), jnp.int32)
    for h in range(N):
        hits = jnp.zeros((N, 128), jnp.int32)
        for d in range(N):
            hits = hits + jnp.where(table[d] == h, 1, 0)
        longest = jnp.maximum(longest, jnp.sum(hits, axis=1, keepdims=True))
    most[...] = longest

    others(lambda i: tile_copy(i, wrap(vm + i)).wait_recv())

    def gather(d, carry):
        for t in range(SLOTS):
            place = spos[d, t]
            piece = zrecv[jnp.maximum(place, 0)]
            piece = jnp.where(place >= 0, piece, jnp.zeros_like(piece))
            comp[d, pl.ds(t, 8, stride=8), :] = piece
        return carry

    lax.fori_loop(0, N, gather, 0)
    through = [jnp.ones((8, 128), jnp.float32)] * 2
    total = [jnp.zeros((8, 128), jnp.float32)] * 8
    for d in range(N):
        part = [comp[d, pl.ds(r * 8, 8), :] for r in range(8)]
        total = [total[r] + through[r // 4] * part[r] for r in range(8)]
        through = [through[pj] * (1.0 - part[pj * 4 + 3]) for pj in range(2)]
    for r in range(8):
        front[pl.ds(r * 8, 8), :] = total[r]
    edges[0] = front[pl.ds(0, 8, stride=8), :]
    edges[1] = front[pl.ds(7, 8, stride=8), :]

    rim = []
    for n, (dd, dv) in enumerate(SIDES):
        if dv == 0 and dd == -1:
            src, dst = front.at[pl.ds(0, 32), :], below
        elif dv == 0:
            src, dst = front.at[pl.ds(32, 32), :], above
        elif dv == 1:
            src, dst = edges.at[1], from_left.at[1 - dd]
        else:
            src, dst = edges.at[0], from_right.at[1 - dd]
        target = (wrap(dm + dd), wrap(vm + dv))
        rim.append(remote(src, dst, rim_send.at[n], rim_recv.at[n], target))
    for copy in rim:
        copy.start()
    for copy in rim:
        copy.wait_recv()

    low = lane8 < 64
    x = lax.rem(lane8, 64)
    upper = sub8 < 4
    nothing = jnp.zeros((8, 128), jnp.float32)

    def mix(before, mid, after):
        return 0.25 * before + 0.5 * mid + 0.25 * after

    def rows_blurred(before, mid, after):
        up = pltpu.roll(jnp.where(low, mid, before), 64, 1)
        down = pltpu.roll(jnp.where(low, after, mid), 64, 1)
        return mix(up, mid, down)

    def edge_blurred(ref, exists):
        top = jnp.where(dm > 0, ref[0], nothing)
        mid = ref[1]
        bottom = jnp.where(dm < N - 1, ref[2], nothing)
        before = pltpu.roll(jnp.where(upper, mid, top), 4, 0)
        after = pltpu.roll(jnp.where(upper, bottom, mid), 4, 0)
        return jnp.where(exists, rows_blurred(before, mid, after), nothing)

    side[0] = pltpu.roll(edge_blurred(from_left, vm > 0), 65, 1)
    side[1] = pltpu.roll(edge_blurred(from_right, vm < N - 1), 63, 1)
    for r in range(8):
        ch = r % 4
        if r < 4:
            before = jnp.where(dm > 0, above[pl.ds(ch * 8, 8), :], nothing)
            after = total[4 + ch]
        else:
            before = total[ch]
            after = jnp.where(dm < N - 1, below[pl.ds(ch * 8, 8), :], nothing)
        rows = rows_blurred(before, total[r], after)
        left_in = jnp.broadcast_to(side[0, pl.ds(r, 1), :], (8, 128))
        right_in = jnp.broadcast_to(side[1, pl.ds(r, 1), :], (8, 128))
        over_left = jnp.where(sub8 == 0, left_in, pltpu.roll(pltpu.roll(rows, 65, 1), 1, 0))
        over_right = jnp.where(sub8 == 7, right_in, pltpu.roll(pltpu.roll(rows, 63, 1), 7, 0))
        left = jnp.where(x == 0, over_left, pltpu.roll(rows, 1, 1))
        right = jnp.where(x == 63, over_right, pltpu.roll(rows, 127, 1))
        blurred = mix(left, rows, right)
        image[pl.ds(r * 8, 8), :] = total[r] + SHARPEN * (total[r] - blurred)

    for copy in rim:
        copy.wait_send()
    others(lambda i: row_copy(i, vm).wait_send())
    others(lambda i: slab_copy(i, dm).wait_send())
    others(lambda i: tile_copy(i, vm).wait_send())

    def drain(k, carry):
        others(lambda i: band_copy(k, i, dm).wait_send())
        return carry

    lax.fori_loop(0, GROUPS, drain, 0)


def fused(tiles, holders):
    f32, i32 = jnp.float32, jnp.int32
    dma = pltpu.SemaphoreType.DMA
    return pl.pallas_call(
        fused_kernel,
        in_specs=[
            pl.BlockSpec(memory_space=pltpu.SMEM),
            pl.BlockSpec(memory_space=pl.ANY),
        ],
        out_specs=(pl.BlockSpec(memory_space=pltpu.VMEM), pl.BlockSpec(memory_space=pltpu.VMEM)),
        out_shape=(jax.ShapeDtypeStruct((64, 128), f32), jax.ShapeDtypeStruct((N, 128), i32)),
        scratch_shapes=[
            pltpu.VMEM((SLOTS, 8, 256, 128), f32),
            pltpu.VMEM((N * SLOTS, 8, 128), f32),
            pltpu.VMEM((N * SLOTS, 8, 128), f32),
            pltpu.VMEM((N * CAP, 8, 128), f32),
            pltpu.VMEM((N * CAP, 8, 128), f32),
            pltpu.VMEM((N, 64, 128), f32),
            pltpu.VMEM((N, 8, 128), i32),
            pltpu.VMEM((N, 128), i32),
            pltpu.VMEM((N, N, 128), i32),
            pltpu.VMEM((N, 128), i32),
            pltpu.VMEM((N, 128), i32),
            pltpu.SMEM((N, 128), i32),
            pltpu.SMEM((N, 128), i32),
            pltpu.VMEM((64, 128), f32),
            pltpu.VMEM((2, 8, 128), f32),
            pltpu.VMEM((32, 128), f32),
            pltpu.VMEM((32, 128), f32),
            pltpu.VMEM((3, 8, 128), f32),
            pltpu.VMEM((3, 8, 128), f32),
            pltpu.VMEM((2, 8, 128), f32),
            dma((SLOTS,)), dma((N,)), dma((N,)), dma((N,)), dma((N,)), dma((2,)),
            dma((GROUPS, N)), dma((GROUPS, N)), dma((N,)), dma((N,)), dma((8,)), dma((8,)),
        ],
        compiler_params=pltpu.CompilerParams(
            collective_id=0, has_side_effects=True, vmem_limit_bytes=40 * 1024 * 1024
        ),
        name="fused",
    )(holders, tiles)


def body(bricks, tile_holder):
    image, most = fused(as_tiles(bricks[0, 0]), tile_holder[0, 0])
    rows = image.reshape(2, 4, SLOTS, 2, 64)
    return rows.transpose(1, 0, 3, 2, 4).reshape(4, 4, SLOTS * 64)


def solution(mesh):
    in_specs = (P("depth", "view", None, None, None), P("depth", "view", None))
    out_specs = P(None, "depth", "view")
    return jax.shard_map(body, mesh=mesh, in_specs=in_specs, out_specs=out_specs, check_vma=False)
```

```python
import math

import jax
import jax.numpy as jnp
from jax import lax
from jax.experimental import pallas as pl
from jax.experimental.pallas import tpu as pltpu
from jax.sharding import PartitionSpec as P

STEPS = 48
DENSITY = 0.8
SHARPEN = 1.5
PERIODS = 16
UNROLL = 4
HALF = DENSITY / STEPS / 2.0
LOG2E = math.log2(math.e)


def render_slot(load, store):
    shape = (8, 128)
    lane = lax.broadcasted_iota(jnp.int32, shape, 1)
    row = lax.broadcasted_iota(jnp.int32, shape, 0)
    x = lax.rem(lane, 64)
    first_x = x == 0
    last_x = x == 63
    low = lane < 64
    top = row == 0
    bottom = row == 7

    def plane_terms(cur):
        out = []
        swapped = [pltpu.roll(c, 64, 1) for c in cur]
        before0 = jnp.where(top, cur[0], pltpu.roll(swapped[3], 1, 0))
        delta = [swapped[0] - before0]
        for g in range(1, 4):
            delta.append(swapped[g] - swapped[g - 1])
        delta.append(jnp.where(bottom, cur[3] - swapped[3], pltpu.roll(delta[0], 7, 0)))
        for g in range(4):
            c = cur[g]
            right = jnp.where(last_x, c, pltpu.roll(c, 127, 1))
            left = jnp.where(first_x, c, pltpu.roll(c, 1, 1))
            gx = right - left
            gy = jnp.where(low, delta[g], delta[g + 1])
            out.append(gx * gx + gy * gy + 36.0)
        return out

    def shade_step(state, cur, plane, behind, ahead):
        trans, acc_a, acc_b, acc_c = state
        new = ([], [], [], [])
        for g in range(4):
            c = cur[g]
            gz = ahead[g] - behind[g]
            slope = jnp.abs(gz) * lax.rsqrt(plane[g] + gz * gz)
            dense = jnp.tanh(c * (1.0 / 3.0) - 2.0)
            kept = jnp.exp2(dense * (-LOG2E * HALF) + (-LOG2E * HALF))
            after = trans[g] * kept
            lit = (trans[g] - after) * (slope + (3.0 / 7.0))
            new[0].append(after)
            new[1].append(acc_a[g] + lit)
            new[2].append(acc_b[g] + lit * jnp.tanh(c * 0.125))
            new[3].append(acc_c[g] + lit * jnp.tanh(c * 0.25 - 1.5))
        return new

    def period_samples(k):
        three = ([], [], [])
        for g in range(4):
            b0, b1, b2, b3 = (load(4 * k + j, g) for j in range(4))
            three[0].append(5.0 * b0 + b1)
            three[1].append(3.0 * (b1 + b2))
            three[2].append(b2 + 5.0 * b3)
        return three

    zeros = [jnp.zeros(shape, jnp.float32)] * 4
    ones = [jnp.ones(shape, jnp.float32)] * 4
    state = (ones, zeros, zeros, zeros)
    p0, p1, p2 = period_samples(0)
    state = shade_step(state, p0, plane_terms(p0), p0, p1)
    state = shade_step(state, p1, plane_terms(p1), p0, p2)
    carry = (p1, p2, plane_terms(p2), state)

    def one_period(k, carry):
        behind, last, last_plane, state = carry
        a, b, c = period_samples(k)
        state = shade_step(state, last, last_plane, behind, a)
        state = shade_step(state, a, plane_terms(a), last, b)
        state = shade_step(state, b, plane_terms(b), a, c)
        return (b, c, plane_terms(c), state)

    carry = lax.fori_loop(1, PERIODS, one_period, carry, unroll=True)
    behind, last, last_plane, state = carry
    trans, acc_a, acc_b, acc_c = shade_step(state, last, last_plane, behind, last)
    for g in range(4):
        store(0, g, 0.35 * (acc_a[g] + acc_b[g]))
        store(1, g, 0.35 * (acc_a[g] - acc_b[g]))
        store(2, g, 0.35 * (acc_a[g] + acc_c[g]))
        store(3, g, 1.0 - trans[g])


def as_tiles(stored):
    slots, edge, pixels = stored.shape
    split = stored.reshape(slots, edge // 8, 8, pixels // 128, 128)
    return split.transpose(0, 1, 3, 2, 4).reshape(slots, edge // 8, pixels // 16, 128)


N = 16
SLOTS = 8
GROUP = 2
GROUPS = SLOTS // GROUP
CAP = 12
MESH = pl.DeviceIdType.MESH
SIDES = [(dd, dv) for dd in (-1, 0, 1) for dv in (-1, 0, 1) if (dd, dv) != (0, 0)]


def wrap(i):
    return lax.rem(i + N, N)


def fused_kernel(
    holders, bricks, image, most, names, buf, dsend, held, zsend, zrecv, comp, row_in, slab, table,
    vidx, vpos, sidx, spos, front, edges, above, below, from_left, from_right, side,
    brick_sem, row_send, row_recv, slab_send, slab_recv, local_sem,
    d_send, d_recv, z_send, z_recv, rim_send, rim_recv,
):
    dm = lax.axis_index("depth")
    vm = lax.axis_index("view")
    lane8 = lax.broadcasted_iota(jnp.int32, (8, 128), 1)
    sub8 = lax.broadcasted_iota(jnp.int32, (8, 128), 0)
    lane16 = lax.broadcasted_iota(jnp.int32, (N, 128), 1)
    sub16 = lax.broadcasted_iota(jnp.int32, (N, 128), 0)

    def remote(src, dst, send, recv, target):
        return pltpu.make_async_remote_copy(
            src_ref=src, dst_ref=dst, send_sem=send, recv_sem=recv,
            device_id=target, device_id_type=MESH,
        )

    def others(step):
        def run(i, carry):
            step(i)
            return carry
        lax.fori_loop(1, N, run, 0)

    barrier = pltpu.get_barrier_semaphore()

    def greet(i):
        pl.semaphore_signal(barrier, inc=1, device_id=(dm, wrap(vm + i)), device_id_type=MESH)
        pl.semaphore_signal(barrier, inc=1, device_id=(wrap(dm + i), vm), device_id_type=MESH)

    others(greet)
    for dd, dv in SIDES:
        if dd != 0 and dv != 0:
            target = (wrap(dm + dd), wrap(vm + dv))
            pl.semaphore_signal(barrier, inc=1, device_id=target, device_id_type=MESH)

    def brick_copy(t):
        return pltpu.make_async_copy(bricks.at[t], buf.at[t], brick_sem.at[t])

    for t in range(SLOTS):
        brick_copy(t).start()
    holder_copy = pltpu.make_async_copy(holders, names, local_sem.at[2])
    holder_copy.start()

    holder_copy.wait()
    mine = jnp.full((8, 128), -1, jnp.int32)
    for t in range(SLOTS):
        mine = jnp.where(lane8 == t, names[0, t], mine)
    row_in[vm] = mine

    def row_copy(i, source):
        return remote(row_in.at[source], row_in.at[source], row_send.at[i], row_recv.at[source],
                      (dm, wrap(vm + i)))

    def render_one(t):
        brick_copy(t).wait()

        def load(z, g):
            return buf[t, z // 8, pl.ds(g * 8 + z % 8, 8, stride=32), :]

        flat = dsend.reshape(N * SLOTS * 8, 128)

        def store(ch, g, value):
            first = ((g // 2) * SLOTS + t) * 8 + (g % 2) * 4 + ch
            flat[pl.ds(first, 8, stride=2 * SLOTS * 8), :] = value

        render_slot(load, store)

    def band_copy(k, i, source):
        target = wrap(dm + i)
        return remote(
            dsend.at[pl.ds(target * SLOTS + k * GROUP, GROUP)],
            held.at[pl.ds(source * SLOTS + k * GROUP, GROUP)],
            d_send.at[k, i], d_recv.at[k, source], (target, vm),
        )

    def slab_copy(i, source):
        return remote(slab, table.at[source], slab_send.at[i], slab_recv.at[source],
                      (wrap(dm + i), vm))

    def render_group(k, carry):
        def one(j, c):
            render_one(k * GROUP + j)
            return c

        lax.fori_loop(0, GROUP, one, 0)
        return send_group(k, c=carry)

    def send_group(k, c):
        others(lambda i: band_copy(k, i, dm).start())
        for j in range(GROUP):
            held[dm * SLOTS + k * GROUP + j] = dsend[dm * SLOTS + k * GROUP + j]
        return c

    def render_first(j, c):
        render_one(j)
        return c

    lax.fori_loop(0, GROUP, render_first, 0)
    pl.semaphore_wait(barrier, 2 * (N - 1) + 4)
    others(lambda i: row_copy(i, vm).start())
    send_group(0, 0)
    lax.fori_loop(1, GROUPS - 1, render_group, 0)
    others(lambda i: row_copy(i, wrap(vm + i)).wait_recv())
    for v in range(N):
        slab[pl.ds(v, 1), :] = row_in[v, pl.ds(0, 1), :]
    table[dm] = slab[...]
    others(lambda i: slab_copy(i, dm).start())
    lax.fori_loop(GROUPS - 1, GROUPS, render_group, 0)

    others(lambda i: slab_copy(i, wrap(dm + i)).wait_recv())
    listed = jnp.zeros((N, 128), jnp.int32)
    count = jnp.zeros((N, 128), jnp.int32)
    for d in range(N):
        slot = jnp.max(jnp.where(table[d] == vm, lane16, -1), axis=1, keepdims=True)
        wanted = slot >= 0
        listed = listed + jnp.where(wanted & (lane16 == count), slot + d * SLOTS, 0)
        count = count + jnp.where(wanted, 1, 0)
    vidx[...] = listed
    index_copy = pltpu.make_async_copy(vidx, sidx, local_sem.at[0])
    index_copy.start()
    index_copy.wait()

    def wait_bands(k, carry):
        others(lambda i: band_copy(k, i, wrap(dm + i)).wait_recv())
        return carry

    lax.fori_loop(0, GROUPS, wait_bands, 0)

    def tile_copy(i, source):
        target = wrap(vm + i)
        return remote(
            zsend.at[pl.ds(target * CAP, CAP)], zrecv.at[pl.ds(source * CAP, CAP)],
            z_send.at[i], z_recv.at[source], (dm, target),
        )

    def pack(i):
        target = wrap(vm + i)
        for j in range(CAP):
            zsend[target * CAP + j] = held[sidx[target, j]]
        tile_copy(i, vm).start()

    others(pack)
    for j in range(CAP):
        zrecv[vm * CAP + j] = held[sidx[vm, j]]

    count = jnp.zeros((N, 128), jnp.int32)
    for d in range(N):
        named = sub16 == table[d, pl.ds(vm, 1), :]
        place = jnp.where(named, sub16 * CAP + count + 1, 0)
        vpos[pl.ds(d, 1), :] = jnp.sum(place, axis=0, keepdims=True) - 1
        count = count + jnp.max(jnp.where(named, 1, 0), axis=1, keepdims=True)
    place_copy = pltpu.make_async_copy(vpos, spos, local_sem.at[1])
    place_copy.start()
    place_copy.wait()

    longest = jnp.zeros((N, 128), jnp.int32)
    for h in range(N):
        hits = jnp.zeros((N, 128), jnp.int32)
        for d in range(N):
            hits = hits + jnp.where(table[d] == h, 1, 0)
        longest = jnp.maximum(longest, jnp.sum(hits, axis=1, keepdims=True))
    most[...] = jnp.broadcast_to(jnp.max(longest, axis=0, keepdims=True), (8, 128))

    others(lambda i: tile_copy(i, wrap(vm + i)).wait_recv())

    def gather(d, carry):
        for t in range(SLOTS):
            place = spos[d, t]
            piece = zrecv[jnp.maximum(place, 0)]
            piece = jnp.where(place >= 0, piece, jnp.zeros_like(piece))
            comp[d, pl.ds(t, 8, stride=8), :] = piece
        return carry

    lax.fori_loop(0, N, gather, 0)
    through = [jnp.ones((8, 128), jnp.float32)] * 2
    total = [jnp.zeros((8, 128), jnp.float32)] * 8
    for d in range(N):
        part = [comp[d, pl.ds(r * 8, 8), :] for r in range(8)]
        total = [total[r] + through[r // 4] * part[r] for r in range(8)]
        through = [through[pj] * (1.0 - part[pj * 4 + 3]) for pj in range(2)]
    for r in range(8):
        front[pl.ds(r * 8, 8), :] = total[r]
    edges[0] = front[pl.ds(0, 8, stride=8), :]
    edges[1] = front[pl.ds(7, 8, stride=8), :]

    rim = []
    for n, (dd, dv) in enumerate(SIDES):
        if dv == 0 and dd == -1:
            src, dst = front.at[pl.ds(0, 32), :], below
        elif dv == 0:
            src, dst = front.at[pl.ds(32, 32), :], above
        elif dv == 1:
            src, dst = edges.at[1], from_left.at[1 - dd]
        else:
            src, dst = edges.at[0], from_right.at[1 - dd]
        target = (wrap(dm + dd), wrap(vm + dv))
        rim.append(remote(src, dst, rim_send.at[n], rim_recv.at[n], target))
    for copy in rim:
        copy.start()
    for copy in rim:
        copy.wait_recv()

    low = lane8 < 64
    x = lax.rem(lane8, 64)
    upper = sub8 < 4
    nothing = jnp.zeros((8, 128), jnp.float32)

    def mix(before, mid, after):
        return 0.25 * before + 0.5 * mid + 0.25 * after

    def rows_blurred(before, mid, after):
        up = pltpu.roll(jnp.where(low, mid, before), 64, 1)
        down = pltpu.roll(jnp.where(low, after, mid), 64, 1)
        return mix(up, mid, down)

    def edge_blurred(ref, exists):
        top = jnp.where(dm > 0, ref[0], nothing)
        mid = ref[1]
        bottom = jnp.where(dm < N - 1, ref[2], nothing)
        before = pltpu.roll(jnp.where(upper, mid, top), 4, 0)
        after = pltpu.roll(jnp.where(upper, bottom, mid), 4, 0)
        return jnp.where(exists, rows_blurred(before, mid, after), nothing)

    side[0] = pltpu.roll(edge_blurred(from_left, vm > 0), 65, 1)
    side[1] = pltpu.roll(edge_blurred(from_right, vm < N - 1), 63, 1)
    for r in range(8):
        ch = r % 4
        if r < 4:
            before = jnp.where(dm > 0, above[pl.ds(ch * 8, 8), :], nothing)
            after = total[4 + ch]
        else:
            before = total[ch]
            after = jnp.where(dm < N - 1, below[pl.ds(ch * 8, 8), :], nothing)
        rows = rows_blurred(before, total[r], after)
        left_in = jnp.broadcast_to(side[0, pl.ds(r, 1), :], (8, 128))
        right_in = jnp.broadcast_to(side[1, pl.ds(r, 1), :], (8, 128))
        over_left = jnp.where(sub8 == 0, left_in, pltpu.roll(pltpu.roll(rows, 65, 1), 1, 0))
        over_right = jnp.where(sub8 == 7, right_in, pltpu.roll(pltpu.roll(rows, 63, 1), 7, 0))
        left = jnp.where(x == 0, over_left, pltpu.roll(rows, 1, 1))
        right = jnp.where(x == 63, over_right, pltpu.roll(rows, 127, 1))
        blurred = mix(left, rows, right)
        image[pl.ds(r * 8, 8), :] = total[r] + SHARPEN * (total[r] - blurred)

    for copy in rim:
        copy.wait_send()
    others(lambda i: row_copy(i, vm).wait_send())
    others(lambda i: slab_copy(i, dm).wait_send())
    others(lambda i: tile_copy(i, vm).wait_send())

    def drain(k, carry):
        others(lambda i: band_copy(k, i, dm).wait_send())
        return carry

    lax.fori_loop(0, GROUPS, drain, 0)


def fused(tiles, holders):
    f32, i32 = jnp.float32, jnp.int32
    dma = pltpu.SemaphoreType.DMA
    return pl.pallas_call(
        fused_kernel,
        in_specs=[
            pl.BlockSpec(memory_space=pl.ANY),
            pl.BlockSpec(memory_space=pl.ANY),
        ],
        out_specs=(pl.BlockSpec(memory_space=pltpu.VMEM), pl.BlockSpec(memory_space=pltpu.VMEM)),
        out_shape=(jax.ShapeDtypeStruct((64, 128), f32), jax.ShapeDtypeStruct((8, 128), i32)),
        scratch_shapes=[
            pltpu.SMEM((1, SLOTS), i32),
            pltpu.VMEM((SLOTS, 8, 256, 128), f32),
            pltpu.VMEM((N * SLOTS, 8, 128), f32),
            pltpu.VMEM((N * SLOTS, 8, 128), f32),
            pltpu.VMEM((N * CAP, 8, 128), f32),
            pltpu.VMEM((N * CAP, 8, 128), f32),
            pltpu.VMEM((N, 64, 128), f32),
            pltpu.VMEM((N, 8, 128), i32),
            pltpu.VMEM((N, 128), i32),
            pltpu.VMEM((N, N, 128), i32),
            pltpu.VMEM((N, 128), i32),
            pltpu.VMEM((N, 128), i32),
            pltpu.SMEM((N, 128), i32),
            pltpu.SMEM((N, 128), i32),
            pltpu.VMEM((64, 128), f32),
            pltpu.VMEM((2, 8, 128), f32),
            pltpu.VMEM((32, 128), f32),
            pltpu.VMEM((32, 128), f32),
            pltpu.VMEM((3, 8, 128), f32),
            pltpu.VMEM((3, 8, 128), f32),
            pltpu.VMEM((2, 8, 128), f32),
            dma((SLOTS,)), dma((N,)), dma((N,)), dma((N,)), dma((N,)), dma((3,)),
            dma((GROUPS, N)), dma((GROUPS, N)), dma((N,)), dma((N,)), dma((8,)), dma((8,)),
        ],
        compiler_params=pltpu.CompilerParams(
            collective_id=0, has_side_effects=True, vmem_limit_bytes=58 * 1024 * 1024
        ),
        name="fused",
    )(holders, tiles)


def render_kernel(bricks_ref, out_ref):
    def load(z, g):
        return bricks_ref[0, z // 8, pl.ds(g * 8 + z % 8, 8, stride=32), :]

    def store(ch, g, value):
        out_ref[0, pl.ds((g // 2) * 8 + ch * 2 + g % 2, 8, stride=16), :] = value

    render_slot(load, store)


def render(bricks):
    slots = bricks.shape[0]
    return pl.pallas_call(
        render_kernel,
        grid=(slots,),
        in_specs=[pl.BlockSpec((1, 8, 256, 128), lambda t: (t, 0, 0, 0))],
        out_specs=pl.BlockSpec((1, 128, 128), lambda t: (t, 0, 0)),
        out_shape=jax.ShapeDtypeStruct((slots, 128, 128), jnp.float32),
        name="render",
    )(bricks)


def padded_2(x, sides, width):
    for axis, dim in sides:
        size, length = (lax.axis_size(axis), x.shape[dim])
        up = [(i, (i + 1) % size) for i in range(size - 1)]
        down = [(j, i) for i, j in up]
        last = lax.slice_in_dim(x, length - width, length, axis=dim)
        initial = lax.slice_in_dim(x, 0, width, axis=dim)
        before = lax.ppermute(last, axis, up)
        after = lax.ppermute(initial, axis, down)
        x = jnp.concatenate([before, x, after], axis=dim)
    return x


def by_collectives(bricks, tile_holder):
    me = lax.axis_index("view")
    tiles = render(as_tiles(bricks[0, 0]))
    table = lax.all_gather(tile_holder[0, 0], "view")
    table = lax.all_gather(table, "depth")
    slot_ids = jnp.arange(8, dtype=jnp.int32)
    slot = jnp.max(jnp.where(table == me, slot_ids, 0), axis=2)
    bands = tiles.reshape(8, 16, 8, 128).transpose(1, 0, 2, 3)
    held = lax.all_to_all(bands, "depth", split_axis=0, concat_axis=0, tiled=True)
    flat = held.reshape(16 * 8, 8, 128)
    index = (jnp.arange(16, dtype=jnp.int32)[None, :] * 8 + slot.T).reshape(-1)
    outgoing = flat[index].reshape(16, 16, 8, 128)
    arrived = lax.all_to_all(outgoing, "view", split_axis=0, concat_axis=0, tiled=True)
    mine = lax.dynamic_index_in_dim(table, me, 1, keepdims=False)
    where_at = jnp.maximum(mine, 0) * 16 + jnp.arange(16, dtype=jnp.int32)[:, None]
    pieces = arrived.reshape(256, 8, 128)[where_at.reshape(-1)].reshape(16, 8, 4, 2, 128)
    pieces = pieces * (mine >= 0).astype(jnp.float32)[:, :, None, None, None]
    current = pieces
    while current.shape[0] > 1:
        pair = current.reshape((current.shape[0] // 2, 2) + current.shape[1:])
        current = pair[:, 0] + (1.0 - pair[:, 0, :, 3:4]) * pair[:, 1]
    merged = current[0]
    block = merged.reshape(8, 4, 4, 64).transpose(1, 2, 0, 3).reshape(4, 4, 512)
    padded = padded_2(block, (("depth", 1), ("view", 2)), 1)
    rows_done = 0.25 * padded[:, :-2] + 0.5 * padded[:, 1:-1] + 0.25 * padded[:, 2:]
    blurred = 0.25 * rows_done[:, :, :-2] + 0.5 * rows_done[:, :, 1:-1] + 0.25 * rows_done[:, :, 2:]
    return block + SHARPEN * (block - blurred)


def body(bricks, tile_holder):
    image, most = fused(as_tiles(bricks[0, 0]), tile_holder[0])
    rows = image.reshape(2, 4, SLOTS, 2, 64)
    block = rows.transpose(1, 0, 3, 2, 4).reshape(4, 4, SLOTS * 64)
    return lax.cond(
        most[0, 0] > CAP, lambda: by_collectives(bricks, tile_holder), lambda: block
    )


def solution(mesh):
    in_specs = (P("depth", "view", None, None, None), P("depth", "view", None))
    out_specs = P(None, "depth", "view")
    return jax.shard_map(body, mesh=mesh, in_specs=in_specs, out_specs=out_specs, check_vma=False)
```

```python
import math

import jax
import jax.numpy as jnp
from jax import lax
from jax.experimental import pallas as pl
from jax.experimental.pallas import tpu as pltpu
from jax.sharding import PartitionSpec as P

STEPS = 48
DENSITY = 0.8
SHARPEN = 1.5
PERIODS = 16
UNROLL = 4
HALF = DENSITY / STEPS / 2.0
LOG2E = math.log2(math.e)


def render_slot(load, store):
    shape = (8, 128)
    lane = lax.broadcasted_iota(jnp.int32, shape, 1)
    row = lax.broadcasted_iota(jnp.int32, shape, 0)
    x = lax.rem(lane, 64)
    first_x = x == 0
    last_x = x == 63
    low = lane < 64
    top = row == 0
    bottom = row == 7

    def plane_terms(cur):
        out = []
        swapped = [pltpu.roll(c, 64, 1) for c in cur]
        before0 = jnp.where(top, cur[0], pltpu.roll(swapped[3], 1, 0))
        delta = [swapped[0] - before0]
        for g in range(1, 4):
            delta.append(swapped[g] - swapped[g - 1])
        delta.append(jnp.where(bottom, cur[3] - swapped[3], pltpu.roll(delta[0], 7, 0)))
        for g in range(4):
            c = cur[g]
            right = jnp.where(last_x, c, pltpu.roll(c, 127, 1))
            left = jnp.where(first_x, c, pltpu.roll(c, 1, 1))
            gx = right - left
            gy = jnp.where(low, delta[g], delta[g + 1])
            out.append(gx * gx + gy * gy + 36.0)
        return out

    def shade_step(state, cur, plane, behind, ahead):
        trans, acc_a, acc_b, acc_c = state
        new = ([], [], [], [])
        for g in range(4):
            c = cur[g]
            gz = ahead[g] - behind[g]
            slope = jnp.abs(gz) * lax.rsqrt(plane[g] + gz * gz)
            dense = jnp.tanh(c * (1.0 / 3.0) - 2.0)
            kept = jnp.exp2(dense * (-LOG2E * HALF) + (-LOG2E * HALF))
            after = trans[g] * kept
            lit = (trans[g] - after) * (slope + (3.0 / 7.0))
            new[0].append(after)
            new[1].append(acc_a[g] + lit)
            new[2].append(acc_b[g] + lit * jnp.tanh(c * 0.125))
            new[3].append(acc_c[g] + lit * jnp.tanh(c * 0.25 - 1.5))
        return new

    def period_samples(k):
        three = ([], [], [])
        for g in range(4):
            b0, b1, b2, b3 = (load(4 * k + j, g) for j in range(4))
            three[0].append(5.0 * b0 + b1)
            three[1].append(3.0 * (b1 + b2))
            three[2].append(b2 + 5.0 * b3)
        return three

    zeros = [jnp.zeros(shape, jnp.float32)] * 4
    ones = [jnp.ones(shape, jnp.float32)] * 4
    state = (ones, zeros, zeros, zeros)
    p0, p1, p2 = period_samples(0)
    state = shade_step(state, p0, plane_terms(p0), p0, p1)
    state = shade_step(state, p1, plane_terms(p1), p0, p2)
    carry = (p1, p2, plane_terms(p2), state)

    def one_period(k, carry):
        behind, last, last_plane, state = carry
        a, b, c = period_samples(k)
        state = shade_step(state, last, last_plane, behind, a)
        state = shade_step(state, a, plane_terms(a), last, b)
        state = shade_step(state, b, plane_terms(b), a, c)
        return (b, c, plane_terms(c), state)

    carry = lax.fori_loop(1, PERIODS, one_period, carry, unroll=True)
    behind, last, last_plane, state = carry
    trans, acc_a, acc_b, acc_c = shade_step(state, last, last_plane, behind, last)
    for g in range(4):
        store(0, g, 0.35 * (acc_a[g] + acc_b[g]))
        store(1, g, 0.35 * (acc_a[g] - acc_b[g]))
        store(2, g, 0.35 * (acc_a[g] + acc_c[g]))
        store(3, g, 1.0 - trans[g])


def as_tiles(stored):
    slots, edge, pixels = stored.shape
    split = stored.reshape(slots, edge // 8, 8, pixels // 128, 128)
    return split.transpose(0, 1, 3, 2, 4).reshape(slots, edge // 8, pixels // 16, 128)


def render_part(load, store, part):
    shape = (8, 128)
    kept_rows = (part, part + 2)
    lane = lax.broadcasted_iota(jnp.int32, shape, 1)
    row = lax.broadcasted_iota(jnp.int32, shape, 0)
    x = lax.rem(lane, 64)
    first_x = x == 0
    last_x = x == 63
    low = lane < 64
    top = row == 0
    bottom = row == 7

    def plane_terms(cur):
        swapped = [pltpu.roll(c, 64, 1) for c in cur]
        if part == 0:
            delta = [swapped[0] - jnp.where(top, cur[0], pltpu.roll(swapped[3], 1, 0))]
        else:
            delta = [None]
        for g in range(1, 4):
            delta.append(swapped[g] - swapped[g - 1])
        if part == 1:
            delta.append(jnp.where(bottom, cur[3], pltpu.roll(swapped[0], 7, 0)) - swapped[3])
        out = []
        for g in kept_rows:
            c = cur[g]
            right = jnp.where(last_x, c, pltpu.roll(c, 127, 1))
            left = jnp.where(first_x, c, pltpu.roll(c, 1, 1))
            gx = right - left
            gy = jnp.where(low, delta[g], delta[g + 1])
            out.append(gx * gx + gy * gy + 36.0)
        return out

    def shade_step(state, cur, plane, behind, ahead):
        trans, acc_a, acc_b, acc_c = state
        new = ([], [], [], [])
        for n, g in enumerate(kept_rows):
            c = cur[g]
            gz = ahead[g] - behind[g]
            slope = jnp.abs(gz) * lax.rsqrt(plane[n] + gz * gz)
            dense = jnp.tanh(c * (1.0 / 3.0) - 2.0)
            kept = jnp.exp2(dense * (-LOG2E * HALF) + (-LOG2E * HALF))
            after = trans[n] * kept
            lit = (trans[n] - after) * (slope + (3.0 / 7.0))
            new[0].append(after)
            new[1].append(acc_a[n] + lit)
            new[2].append(acc_b[n] + lit * jnp.tanh(c * 0.125))
            new[3].append(acc_c[n] + lit * jnp.tanh(c * 0.25 - 1.5))
        return new

    def period_samples(k):
        three = ([], [], [])
        for g in range(4):
            b0, b1, b2, b3 = (load(4 * k + j, g) for j in range(4))
            three[0].append(5.0 * b0 + b1)
            three[1].append(3.0 * (b1 + b2))
            three[2].append(b2 + 5.0 * b3)
        return three

    zeros = [jnp.zeros(shape, jnp.float32)] * 2
    ones = [jnp.ones(shape, jnp.float32)] * 2
    state = (ones, zeros, zeros, zeros)
    p0, p1, p2 = period_samples(0)
    state = shade_step(state, p0, plane_terms(p0), p0, p1)
    state = shade_step(state, p1, plane_terms(p1), p0, p2)
    carry = (p1, p2, plane_terms(p2), state)

    def one_period(k, carry):
        behind, last, last_plane, state = carry
        a, b, c = period_samples(k)
        state = shade_step(state, last, last_plane, behind, a)
        state = shade_step(state, a, plane_terms(a), last, b)
        state = shade_step(state, b, plane_terms(b), a, c)
        return (b, c, plane_terms(c), state)

    carry = lax.fori_loop(1, PERIODS, one_period, carry, unroll=True)
    behind, last, last_plane, state = carry
    trans, acc_a, acc_b, acc_c = shade_step(state, last, last_plane, behind, last)
    for n, g in enumerate(kept_rows):
        store(0, g, 0.35 * (acc_a[n] + acc_b[n]))
        store(1, g, 0.35 * (acc_a[n] - acc_b[n]))
        store(2, g, 0.35 * (acc_a[n] + acc_c[n]))
        store(3, g, 1.0 - trans[n])


N = 16
SLOTS = 8
PAIRS = SLOTS // 2
GROUPS = 2
GROUP = SLOTS // GROUPS
CAP = 12
MESH = pl.DeviceIdType.MESH
SIDES = [(dd, dv) for dd in (-1, 0, 1) for dv in (-1, 0, 1) if (dd, dv) != (0, 0)]


def wrap(i):
    return lax.rem(i + N, N)


def fused_kernel(
    holders, bricks, image, most, names, buf, dsend, held0, held1, zsend, zrecv0, zrecv1, comp, row_in, slab, table,
    vidx, vpos, sidx, spos, front, edges, above, below, from_left, from_right, side,
    brick_sem, row_send, row_recv, slab_send, slab_recv, local_sem,
    d_send, d_recv, z_send, z_recv, rim_send, rim_recv,
):
    dm = lax.axis_index("depth")
    vm = lax.axis_index("view")
    held = (held0, held1)
    zrecv = (zrecv0, zrecv1)
    lane8 = lax.broadcasted_iota(jnp.int32, (8, 128), 1)
    sub8 = lax.broadcasted_iota(jnp.int32, (8, 128), 0)
    lane16 = lax.broadcasted_iota(jnp.int32, (N, 128), 1)
    sub16 = lax.broadcasted_iota(jnp.int32, (N, 128), 0)

    def remote(src, dst, send, recv, target):
        return pltpu.make_async_remote_copy(
            src_ref=src, dst_ref=dst, send_sem=send, recv_sem=recv,
            device_id=target, device_id_type=MESH,
        )

    def others(step):
        def run(i, carry):
            step(i)
            return carry
        lax.fori_loop(1, N, run, 0)

    barrier = pltpu.get_barrier_semaphore()

    def greet(i):
        pl.semaphore_signal(barrier, inc=1, device_id=(dm, wrap(vm + i)), device_id_type=MESH)
        pl.semaphore_signal(barrier, inc=1, device_id=(wrap(dm + i), vm), device_id_type=MESH)

    others(greet)
    for dd, dv in SIDES:
        if dd != 0 and dv != 0:
            target = (wrap(dm + dd), wrap(vm + dv))
            pl.semaphore_signal(barrier, inc=1, device_id=target, device_id_type=MESH)

    def brick_copy(t, g):
        return pltpu.make_async_copy(bricks.at[t, :, :, g], buf.at[t, g], brick_sem.at[t, g])

    for t in range(SLOTS):
        for g in range(4):
            brick_copy(t, g).start()
    holder_copy = pltpu.make_async_copy(holders, names, local_sem.at[2])
    holder_copy.start()

    holder_copy.wait()
    mine = jnp.full((8, 128), -1, jnp.int32)
    for t in range(SLOTS):
        mine = jnp.where(lane8 == t, names[0, t], mine)
    row_in[vm] = mine

    def row_copy(i, source):
        return remote(row_in.at[source], row_in.at[source], row_send.at[i], row_recv.at[source],
                      (dm, wrap(vm + i)))

    def render_one(part, t):
        if part == 0:
            for g in range(4):
                brick_copy(t, g).wait()
        voxels = buf.reshape(SLOTS * 4 * 8 * 64, 128)

        def load(z, g):
            first = ((t * 4 + g) * 8 + z // 8) * 64 + z % 8
            return voxels[pl.ds(first, 8, stride=8), :]

        flat = dsend.reshape(2 * N * PAIRS * 8, 128)

        def store(ch, g, value):
            first = part * N * SLOTS * 4 + ((g // 2) * SLOTS + t) * 4 + ch
            flat[pl.ds(first, 8, stride=2 * SLOTS * 4), :] = value

        render_part(load, store, part)

    def band_copy(part, k, i, source):
        target = wrap(dm + i)
        blocks = GROUP // 2
        return remote(
            dsend.at[part, pl.ds(target * PAIRS + k * blocks, blocks)],
            held[part].at[pl.ds(source * PAIRS + k * blocks, blocks)],
            d_send.at[part * GROUPS + k, i], d_recv.at[part * GROUPS + k, source], (target, vm),
        )

    def slab_copy(i, source):
        return remote(slab, table.at[source], slab_send.at[i], slab_recv.at[source],
                      (wrap(dm + i), vm))

    def send_bands(part, k):
        others(lambda i: band_copy(part, k, i, dm).start())
        for j in range(GROUP // 2):
            block = dm * PAIRS + k * (GROUP // 2) + j
            held[part][block] = dsend[part, block]

    def wait_bands(part):
        for k in range(GROUPS):
            others(lambda i: band_copy(part, k, i, wrap(dm + i)).wait_recv())

    half = CAP // 2

    def tile_copy(part, i, source):
        target = wrap(vm + i)
        return remote(
            zsend.at[part, pl.ds(target * half, half)], zrecv[part].at[pl.ds(source * half, half)],
            z_send.at[part, i], z_recv.at[part, source], (dm, target),
        )

    first_rows = sub8 < 4

    def two_pieces(part, target, j):
        a = sidx[target, 2 * j]
        b = sidx[target, 2 * j + 1]
        x = held[part][a >> 1]
        y = held[part][b >> 1]
        x = jnp.where((a & 1) == 1, pltpu.roll(x, 4, 0), x)
        y = jnp.where((b & 1) == 1, y, pltpu.roll(y, 4, 0))
        return jnp.where(first_rows, x, y)

    def send_tiles(part):
        def pack(i):
            target = wrap(vm + i)
            for j in range(half):
                zsend[part, target * half + j] = two_pieces(part, target, j)
            tile_copy(part, i, vm).start()

        others(pack)
        for j in range(half):
            zrecv[part][vm * half + j] = two_pieces(part, vm, j)

    def list_tiles():
        others(lambda i: slab_copy(i, wrap(dm + i)).wait_recv())
        listed = jnp.zeros((N, 128), jnp.int32)
        count = jnp.zeros((N, 128), jnp.int32)
        for d in range(N):
            slot = jnp.max(jnp.where(table[d] == vm, lane16, -1), axis=1, keepdims=True)
            wanted = slot >= 0
            listed = listed + jnp.where(wanted & (lane16 == count), slot + d * SLOTS, 0)
            count = count + jnp.where(wanted, 1, 0)
        vidx[...] = listed
        index_copy().start()

    def index_copy():
        return pltpu.make_async_copy(vidx, sidx, local_sem.at[0])

    def early(t, carry):
        render_one(0, t)

        @pl.when(t == 1)
        def _():
            pl.semaphore_wait(barrier, 2 * (N - 1) + 4)
            others(lambda i: row_copy(i, vm).start())

        for k in range(GROUPS):
            @pl.when(t == (k + 1) * GROUP - 1)
            def _(k=k):
                send_bands(0, k)

        return carry

    lax.fori_loop(0, SLOTS, early, 0)
    others(lambda i: row_copy(i, wrap(vm + i)).wait_recv())
    for v in range(N):
        slab[pl.ds(v, 1), :] = row_in[v, pl.ds(0, 1), :]
    table[dm] = slab[...]
    others(lambda i: slab_copy(i, dm).start())

    def late(t, carry):
        render_one(1, t)
        for k in range(GROUPS):
            @pl.when(t == (k + 1) * GROUP - 1)
            def _(k=k):
                send_bands(1, k)

        @pl.when(t == SLOTS - 4)
        def _():
            list_tiles()

        @pl.when(t == SLOTS - 3)
        def _():
            index_copy().wait()
            wait_bands(0)
            send_tiles(0)

        return carry

    lax.fori_loop(0, SLOTS, late, 0)
    wait_bands(1)
    send_tiles(1)

    count = jnp.zeros((N, 128), jnp.int32)
    for d in range(N):
        named = sub16 == table[d, pl.ds(vm, 1), :]
        place = jnp.where(named, sub16 * CAP + count + 1, 0)
        vpos[pl.ds(d, 1), :] = jnp.sum(place, axis=0, keepdims=True) - 1
        count = count + jnp.max(jnp.where(named, 1, 0), axis=1, keepdims=True)
    place_copy = pltpu.make_async_copy(vpos, spos, local_sem.at[1])
    place_copy.start()
    place_copy.wait()

    longest = jnp.zeros((N, 128), jnp.int32)
    for h in range(N):
        hits = jnp.zeros((N, 128), jnp.int32)
        for d in range(N):
            hits = hits + jnp.where(table[d] == h, 1, 0)
        longest = jnp.maximum(longest, jnp.sum(hits, axis=1, keepdims=True))
    most[...] = jnp.broadcast_to(jnp.max(longest, axis=0, keepdims=True), (8, 128))

    def compose(part):
        others(lambda i: tile_copy(part, i, wrap(vm + i)).wait_recv())

        def gather(d, carry):
            for t in range(SLOTS):
                place = spos[d, t]
                safe = jnp.maximum(place, 0)
                piece = zrecv[part][safe >> 1]
                piece = jnp.where((safe & 1) == 1, pltpu.roll(piece, 4, 0), piece)
                piece = jnp.where(place >= 0, piece, jnp.zeros_like(piece))
                comp[d, pl.ds(t, 4, stride=8), :] = piece[0:4]
            return carry

        lax.fori_loop(0, N, gather, 0)
        through = jnp.ones((8, 128), jnp.float32)
        sums = [jnp.zeros((8, 128), jnp.float32)] * 4
        for d in range(N):
            layer = [comp[d, pl.ds(ch * 8, 8), :] for ch in range(4)]
            sums = [sums[ch] + through * layer[ch] for ch in range(4)]
            through = through * (1.0 - layer[3])
        return sums

    total = compose(0) + compose(1)
    for r in range(8):
        front[pl.ds(r * 8, 8), :] = total[r]
    edges[0] = front[pl.ds(0, 8, stride=8), :]
    edges[1] = front[pl.ds(7, 8, stride=8), :]

    rim = []
    for n, (dd, dv) in enumerate(SIDES):
        if dv == 0 and dd == -1:
            src, dst = front.at[pl.ds(0, 32), :], below
        elif dv == 0:
            src, dst = front.at[pl.ds(32, 32), :], above
        elif dv == 1:
            src, dst = edges.at[1], from_left.at[1 - dd]
        else:
            src, dst = edges.at[0], from_right.at[1 - dd]
        target = (wrap(dm + dd), wrap(vm + dv))
        rim.append(remote(src, dst, rim_send.at[n], rim_recv.at[n], target))
    for copy in rim:
        copy.start()
    for copy in rim:
        copy.wait_recv()

    low = lane8 < 64
    x = lax.rem(lane8, 64)
    upper = sub8 < 4
    nothing = jnp.zeros((8, 128), jnp.float32)

    def mix(before, mid, after):
        return 0.25 * before + 0.5 * mid + 0.25 * after

    def rows_blurred(before, mid, after):
        up = pltpu.roll(jnp.where(low, mid, before), 64, 1)
        down = pltpu.roll(jnp.where(low, after, mid), 64, 1)
        return mix(up, mid, down)

    def edge_blurred(ref, exists):
        top = jnp.where(dm > 0, ref[0], nothing)
        mid = ref[1]
        bottom = jnp.where(dm < N - 1, ref[2], nothing)
        before = pltpu.roll(jnp.where(upper, mid, top), 4, 0)
        after = pltpu.roll(jnp.where(upper, bottom, mid), 4, 0)
        return jnp.where(exists, rows_blurred(before, mid, after), nothing)

    for copy in rim:
        copy.wait_send()
    side[0] = pltpu.roll(edge_blurred(from_left, vm > 0), 65, 1)
    side[1] = pltpu.roll(edge_blurred(from_right, vm < N - 1), 63, 1)
    for r in range(8):
        ch = r % 4
        if r < 4:
            before = jnp.where(dm > 0, above[pl.ds(ch * 8, 8), :], nothing)
            after = total[4 + ch]
        else:
            before = total[ch]
            after = jnp.where(dm < N - 1, below[pl.ds(ch * 8, 8), :], nothing)
        rows = rows_blurred(before, total[r], after)
        left_in = jnp.broadcast_to(side[0, pl.ds(r, 1), :], (8, 128))
        right_in = jnp.broadcast_to(side[1, pl.ds(r, 1), :], (8, 128))
        over_left = jnp.where(sub8 == 0, left_in, pltpu.roll(pltpu.roll(rows, 65, 1), 1, 0))
        over_right = jnp.where(sub8 == 7, right_in, pltpu.roll(pltpu.roll(rows, 63, 1), 7, 0))
        left = jnp.where(x == 0, over_left, pltpu.roll(rows, 1, 1))
        right = jnp.where(x == 63, over_right, pltpu.roll(rows, 127, 1))
        blurred = mix(left, rows, right)
        front[pl.ds(r * 8, 8), :] = total[r] + SHARPEN * (total[r] - blurred)
    for r in range(8):
        pj, ch = divmod(r, 4)
        even = front[pl.ds(r * 8, 4, stride=2), :]
        odd = front[pl.ds(r * 8 + 1, 4, stride=2), :]
        row0 = jnp.where(low[0:4], even, pltpu.roll(odd, 64, 1))
        row1 = jnp.where(low[0:4], pltpu.roll(even, 64, 1), odd)
        for m in range(4):
            image[ch, pl.ds(2 * pj, 1), pl.ds(m * 128, 128)] = row0[m:m + 1]
            image[ch, pl.ds(2 * pj + 1, 1), pl.ds(m * 128, 128)] = row1[m:m + 1]

    others(lambda i: row_copy(i, vm).wait_send())
    others(lambda i: slab_copy(i, dm).wait_send())
    for part in range(2):
        others(lambda i: tile_copy(part, i, vm).wait_send())
        for k in range(GROUPS):
            others(lambda i: band_copy(part, k, i, dm).wait_send())


def fused(tiles, holders):
    f32, i32 = jnp.float32, jnp.int32
    dma = pltpu.SemaphoreType.DMA
    return pl.pallas_call(
        fused_kernel,
        in_specs=[
            pl.BlockSpec(memory_space=pl.ANY),
            pl.BlockSpec(memory_space=pl.ANY),
        ],
        out_specs=(pl.BlockSpec(memory_space=pltpu.VMEM), pl.BlockSpec(memory_space=pltpu.VMEM)),
        out_shape=(jax.ShapeDtypeStruct((4, 4, SLOTS * 64), f32), jax.ShapeDtypeStruct((8, 128), i32)),
        scratch_shapes=[
            pltpu.SMEM((1, SLOTS), i32),
            pltpu.VMEM((SLOTS, 4, 8, 8, 8, 128), f32),
            pltpu.VMEM((2, N * PAIRS, 8, 128), f32),
            pltpu.VMEM((N * PAIRS, 8, 128), f32),
            pltpu.VMEM((N * PAIRS, 8, 128), f32),
            pltpu.VMEM((2, N * CAP // 2, 8, 128), f32),
            pltpu.VMEM((N * CAP // 2, 8, 128), f32),
            pltpu.VMEM((N * CAP // 2, 8, 128), f32),
            pltpu.VMEM((N, 32, 128), f32),
            pltpu.VMEM((N, 8, 128), i32),
            pltpu.VMEM((N, 128), i32),
            pltpu.VMEM((N, N, 128), i32),
            pltpu.VMEM((N, 128), i32),
            pltpu.VMEM((N, 128), i32),
            pltpu.SMEM((N, 128), i32),
            pltpu.SMEM((N, 128), i32),
            pltpu.VMEM((64, 128), f32),
            pltpu.VMEM((2, 8, 128), f32),
            pltpu.VMEM((32, 128), f32),
            pltpu.VMEM((32, 128), f32),
            pltpu.VMEM((3, 8, 128), f32),
            pltpu.VMEM((3, 8, 128), f32),
            pltpu.VMEM((2, 8, 128), f32),
            dma((SLOTS, 4)), dma((N,)), dma((N,)), dma((N,)), dma((N,)), dma((3,)),
            dma((2 * GROUPS, N)), dma((2 * GROUPS, N)), dma((2, N)), dma((2, N)), dma((8,)), dma((8,)),
        ],
        compiler_params=pltpu.CompilerParams(
            collective_id=0, has_side_effects=True, vmem_limit_bytes=58 * 1024 * 1024
        ),
        name="fused",
    )(holders, tiles)


def render_kernel(bricks_ref, out_ref):
    def load(z, g):
        return bricks_ref[0, z // 8, pl.ds(g * 8 + z % 8, 8, stride=32), :]

    def store(ch, g, value):
        out_ref[0, pl.ds((g // 2) * 8 + ch * 2 + g % 2, 8, stride=16), :] = value

    render_slot(load, store)


def render(bricks):
    slots = bricks.shape[0]
    return pl.pallas_call(
        render_kernel,
        grid=(slots,),
        in_specs=[pl.BlockSpec((1, 8, 256, 128), lambda t: (t, 0, 0, 0))],
        out_specs=pl.BlockSpec((1, 128, 128), lambda t: (t, 0, 0)),
        out_shape=jax.ShapeDtypeStruct((slots, 128, 128), jnp.float32),
        name="render",
    )(bricks)


def padded_2(x, sides, width):
    for axis, dim in sides:
        size, length = (lax.axis_size(axis), x.shape[dim])
        up = [(i, (i + 1) % size) for i in range(size - 1)]
        down = [(j, i) for i, j in up]
        last = lax.slice_in_dim(x, length - width, length, axis=dim)
        initial = lax.slice_in_dim(x, 0, width, axis=dim)
        before = lax.ppermute(last, axis, up)
        after = lax.ppermute(initial, axis, down)
        x = jnp.concatenate([before, x, after], axis=dim)
    return x


def by_collectives(bricks, tile_holder):
    me = lax.axis_index("view")
    tiles = render(as_tiles(bricks[0, 0]))
    table = lax.all_gather(tile_holder[0, 0], "view")
    table = lax.all_gather(table, "depth")
    slot_ids = jnp.arange(8, dtype=jnp.int32)
    slot = jnp.max(jnp.where(table == me, slot_ids, 0), axis=2)
    bands = tiles.reshape(8, 16, 8, 128).transpose(1, 0, 2, 3)
    held = lax.all_to_all(bands, "depth", split_axis=0, concat_axis=0, tiled=True)
    flat = held.reshape(16 * 8, 8, 128)
    index = (jnp.arange(16, dtype=jnp.int32)[None, :] * 8 + slot.T).reshape(-1)
    outgoing = flat[index].reshape(16, 16, 8, 128)
    arrived = lax.all_to_all(outgoing, "view", split_axis=0, concat_axis=0, tiled=True)
    mine = lax.dynamic_index_in_dim(table, me, 1, keepdims=False)
    where_at = jnp.maximum(mine, 0) * 16 + jnp.arange(16, dtype=jnp.int32)[:, None]
    pieces = arrived.reshape(256, 8, 128)[where_at.reshape(-1)].reshape(16, 8, 4, 2, 128)
    pieces = pieces * (mine >= 0).astype(jnp.float32)[:, :, None, None, None]
    current = pieces
    while current.shape[0] > 1:
        pair = current.reshape((current.shape[0] // 2, 2) + current.shape[1:])
        current = pair[:, 0] + (1.0 - pair[:, 0, :, 3:4]) * pair[:, 1]
    merged = current[0]
    block = merged.reshape(8, 4, 4, 64).transpose(1, 2, 0, 3).reshape(4, 4, 512)
    padded = padded_2(block, (("depth", 1), ("view", 2)), 1)
    rows_done = 0.25 * padded[:, :-2] + 0.5 * padded[:, 1:-1] + 0.25 * padded[:, 2:]
    blurred = 0.25 * rows_done[:, :, :-2] + 0.5 * rows_done[:, :, 1:-1] + 0.25 * rows_done[:, :, 2:]
    return block + SHARPEN * (block - blurred)


def body(bricks, tile_holder):
    tiles = as_tiles(bricks[0, 0]).reshape(SLOTS, 8, 8, 4, 8, 128)
    image, most = fused(tiles, tile_holder[0])
    return lax.cond(
        most[0, 0] > CAP, lambda: by_collectives(bricks, tile_holder), lambda: image
    )


def solution(mesh):
    in_specs = (P("depth", "view", None, None, None), P("depth", "view", None))
    out_specs = P(None, "depth", "view")
    return jax.shard_map(body, mesh=mesh, in_specs=in_specs, out_specs=out_specs, check_vma=False)
```

```python
import math

import jax
import jax.numpy as jnp
from jax import lax
from jax.experimental import pallas as pl
from jax.experimental.pallas import tpu as pltpu
from jax.sharding import PartitionSpec as P

STEPS = 48
DENSITY = 0.8
SHARPEN = 1.5
PERIODS = 16
UNROLL = 4
HALF = DENSITY / STEPS / 2.0
LOG2E = math.log2(math.e)


def render_slot(load, store):
    shape = (8, 128)
    lane = lax.broadcasted_iota(jnp.int32, shape, 1)
    row = lax.broadcasted_iota(jnp.int32, shape, 0)
    x = lax.rem(lane, 64)
    first_x = x == 0
    last_x = x == 63
    low = lane < 64
    top = row == 0
    bottom = row == 7

    def plane_terms(cur):
        out = []
        swapped = [pltpu.roll(c, 64, 1) for c in cur]
        before0 = jnp.where(top, cur[0], pltpu.roll(swapped[3], 1, 0))
        delta = [swapped[0] - before0]
        for g in range(1, 4):
            delta.append(swapped[g] - swapped[g - 1])
        delta.append(jnp.where(bottom, cur[3] - swapped[3], pltpu.roll(delta[0], 7, 0)))
        for g in range(4):
            c = cur[g]
            right = jnp.where(last_x, c, pltpu.roll(c, 127, 1))
            left = jnp.where(first_x, c, pltpu.roll(c, 1, 1))
            gx = right - left
            gy = jnp.where(low, delta[g], delta[g + 1])
            out.append(gx * gx + gy * gy + 36.0)
        return out

    def shade_step(state, cur, plane, behind, ahead):
        trans, acc_a, acc_b, acc_c = state
        new = ([], [], [], [])
        for g in range(4):
            c = cur[g]
            gz = ahead[g] - behind[g]
            slope = jnp.abs(gz) * lax.rsqrt(plane[g] + gz * gz)
            dense = jnp.tanh(c * (1.0 / 3.0) - 2.0)
            kept = jnp.exp2(dense * (-LOG2E * HALF) + (-LOG2E * HALF))
            after = trans[g] * kept
            lit = (trans[g] - after) * (slope + (3.0 / 7.0))
            new[0].append(after)
            new[1].append(acc_a[g] + lit)
            new[2].append(acc_b[g] + lit * jnp.tanh(c * 0.125))
            new[3].append(acc_c[g] + lit * jnp.tanh(c * 0.25 - 1.5))
        return new

    def period_samples(k):
        three = ([], [], [])
        for g in range(4):
            b0, b1, b2, b3 = (load(4 * k + j, g) for j in range(4))
            three[0].append(5.0 * b0 + b1)
            three[1].append(3.0 * (b1 + b2))
            three[2].append(b2 + 5.0 * b3)
        return three

    zeros = [jnp.zeros(shape, jnp.float32)] * 4
    ones = [jnp.ones(shape, jnp.float32)] * 4
    state = (ones, zeros, zeros, zeros)
    p0, p1, p2 = period_samples(0)
    state = shade_step(state, p0, plane_terms(p0), p0, p1)
    state = shade_step(state, p1, plane_terms(p1), p0, p2)
    carry = (p1, p2, plane_terms(p2), state)

    def one_period(k, carry):
        behind, last, last_plane, state = carry
        a, b, c = period_samples(k)
        state = shade_step(state, last, last_plane, behind, a)
        state = shade_step(state, a, plane_terms(a), last, b)
        state = shade_step(state, b, plane_terms(b), a, c)
        return (b, c, plane_terms(c), state)

    carry = lax.fori_loop(1, PERIODS, one_period, carry, unroll=True)
    behind, last, last_plane, state = carry
    trans, acc_a, acc_b, acc_c = shade_step(state, last, last_plane, behind, last)
    for g in range(4):
        store(0, g, 0.35 * (acc_a[g] + acc_b[g]))
        store(1, g, 0.35 * (acc_a[g] - acc_b[g]))
        store(2, g, 0.35 * (acc_a[g] + acc_c[g]))
        store(3, g, 1.0 - trans[g])


def as_tiles(stored):
    slots, edge, pixels = stored.shape
    split = stored.reshape(slots, edge // 8, 8, pixels // 128, 128)
    return split.transpose(0, 1, 3, 2, 4).reshape(slots, edge // 8, pixels // 16, 128)


def render_part(load, store, part):
    shape = (8, 128)
    kept_rows = (part, part + 2)
    lane = lax.broadcasted_iota(jnp.int32, shape, 1)
    row = lax.broadcasted_iota(jnp.int32, shape, 0)
    x = lax.rem(lane, 64)
    first_x = x == 0
    last_x = x == 63
    low = lane < 64
    top = row == 0
    bottom = row == 7

    def plane_terms(cur):
        swapped = [pltpu.roll(c, 64, 1) for c in cur]
        if part == 0:
            delta = [swapped[0] - jnp.where(top, cur[0], pltpu.roll(swapped[3], 1, 0))]
        else:
            delta = [None]
        for g in range(1, 4):
            delta.append(swapped[g] - swapped[g - 1])
        if part == 1:
            delta.append(jnp.where(bottom, cur[3], pltpu.roll(swapped[0], 7, 0)) - swapped[3])
        out = []
        for g in kept_rows:
            c = cur[g]
            right = jnp.where(last_x, c, pltpu.roll(c, 127, 1))
            left = jnp.where(first_x, c, pltpu.roll(c, 1, 1))
            gx = right - left
            gy = jnp.where(low, delta[g], delta[g + 1])
            out.append(gx * gx + gy * gy + 36.0)
        return out

    def shade_step(state, cur, plane, behind, ahead):
        trans, acc_a, acc_b, acc_c = state
        new = ([], [], [], [])
        for n, g in enumerate(kept_rows):
            c = cur[g]
            gz = ahead[g] - behind[g]
            slope = jnp.abs(gz) * lax.rsqrt(plane[n] + gz * gz)
            dense = jnp.tanh(c * (1.0 / 3.0) - 2.0)
            kept = jnp.exp2(dense * (-LOG2E * HALF) + (-LOG2E * HALF))
            after = trans[n] * kept
            lit = (trans[n] - after) * (slope + (3.0 / 7.0))
            new[0].append(after)
            new[1].append(acc_a[n] + lit)
            new[2].append(acc_b[n] + lit * jnp.tanh(c * 0.125))
            new[3].append(acc_c[n] + lit * jnp.tanh(c * 0.25 - 1.5))
        return new

    def period_samples(k):
        three = ([], [], [])
        for g in range(4):
            b0, b1, b2, b3 = (load(4 * k + j, g) for j in range(4))
            three[0].append(5.0 * b0 + b1)
            three[1].append(3.0 * (b1 + b2))
            three[2].append(b2 + 5.0 * b3)
        return three

    zeros = [jnp.zeros(shape, jnp.float32)] * 2
    ones = [jnp.ones(shape, jnp.float32)] * 2
    state = (ones, zeros, zeros, zeros)
    p0, p1, p2 = period_samples(0)
    state = shade_step(state, p0, plane_terms(p0), p0, p1)
    state = shade_step(state, p1, plane_terms(p1), p0, p2)
    carry = (p1, p2, plane_terms(p2), state)

    def one_period(k, carry):
        behind, last, last_plane, state = carry
        a, b, c = period_samples(k)
        state = shade_step(state, last, last_plane, behind, a)
        state = shade_step(state, a, plane_terms(a), last, b)
        state = shade_step(state, b, plane_terms(b), a, c)
        return (b, c, plane_terms(c), state)

    carry = lax.fori_loop(1, PERIODS, one_period, carry, unroll=True)
    behind, last, last_plane, state = carry
    trans, acc_a, acc_b, acc_c = shade_step(state, last, last_plane, behind, last)
    for n, g in enumerate(kept_rows):
        store(0, g, 0.35 * (acc_a[n] + acc_b[n]))
        store(1, g, 0.35 * (acc_a[n] - acc_b[n]))
        store(2, g, 0.35 * (acc_a[n] + acc_c[n]))
        store(3, g, 1.0 - trans[n])


N = 16
SLOTS = 8
PAIRS = SLOTS // 2
GROUPS = 2
GROUP = SLOTS // GROUPS
CHIPS = N // 2
CAP = 20
MESH = pl.DeviceIdType.MESH
SIDES = [(dd, dv) for dd in (-1, 0, 1) for dv in (-1, 0, 1) if (dd, dv) != (0, 0)]


def wrap(i):
    return lax.rem(i + N, N)


def fused_kernel(
    holders, bricks, image, most, names, buf, dsend, held0, held1, zsend, zrecv0, zrecv1, comp, row_in, slab, table,
    vidx, vpos, sidx, spos, front, edges, above, below, from_left, from_right, side,
    pass_send, pass_recv, brick_sem, row_send, row_recv, slab_send, slab_recv, local_sem,
    d_send, d_recv, z_send, z_recv, rim_send, rim_recv,
):
    dm = lax.axis_index("depth")
    vm = lax.axis_index("view")
    held = (held0, held1)
    chip = vm // 2
    core = lax.rem(vm, 2)
    zrecv = (zrecv0, zrecv1)
    lane8 = lax.broadcasted_iota(jnp.int32, (8, 128), 1)
    sub8 = lax.broadcasted_iota(jnp.int32, (8, 128), 0)
    lane16 = lax.broadcasted_iota(jnp.int32, (N, 128), 1)
    sub16 = lax.broadcasted_iota(jnp.int32, (N, 128), 0)
    second = lax.rem(sub16, 2) == 1

    def partner_row(x):
        return jnp.where(second, pltpu.roll(x, 1, 0), pltpu.roll(x, N - 1, 0))

    def remote(src, dst, send, recv, target):
        return pltpu.make_async_remote_copy(
            src_ref=src, dst_ref=dst, send_sem=send, recv_sem=recv,
            device_id=target, device_id_type=MESH,
        )

    def others(step):
        def run(i, carry):
            step(i)
            return carry
        lax.fori_loop(1, N, run, 0)

    barrier = pltpu.get_barrier_semaphore()

    def greet(i):
        pl.semaphore_signal(barrier, inc=1, device_id=(dm, wrap(vm + i)), device_id_type=MESH)
        pl.semaphore_signal(barrier, inc=1, device_id=(wrap(dm + i), vm), device_id_type=MESH)

    others(greet)
    for dd, dv in SIDES:
        if dd != 0 and dv != 0:
            target = (wrap(dm + dd), wrap(vm + dv))
            pl.semaphore_signal(barrier, inc=1, device_id=target, device_id_type=MESH)

    def brick_copy(t, g):
        return pltpu.make_async_copy(bricks.at[t, :, :, g], buf.at[t, g], brick_sem.at[t, g])

    for t in range(SLOTS):
        for g in range(4):
            brick_copy(t, g).start()
    holder_copy = pltpu.make_async_copy(holders, names, local_sem.at[2])
    holder_copy.start()

    holder_copy.wait()
    mine = jnp.full((8, 128), -1, jnp.int32)
    for t in range(SLOTS):
        mine = jnp.where(lane8 == t, names[0, t], mine)
    row_in[vm] = mine

    def row_copy(i, source):
        return remote(row_in.at[source], row_in.at[source], row_send.at[i], row_recv.at[source],
                      (dm, wrap(vm + i)))

    def render_one(part, t):
        if part == 0:
            for g in range(4):
                brick_copy(t, g).wait()
        voxels = buf.reshape(SLOTS * 4 * 8 * 64, 128)

        def load(z, g):
            first = ((t * 4 + g) * 8 + z // 8) * 64 + z % 8
            return voxels[pl.ds(first, 8, stride=8), :]

        flat = dsend.reshape(2 * N * PAIRS * 8, 128)

        def store(ch, g, value):
            first = part * N * SLOTS * 4 + ((g // 2) * SLOTS + t) * 4 + ch
            flat[pl.ds(first, 8, stride=2 * SLOTS * 4), :] = value

        render_part(load, store, part)

    def band_copy(part, k, i, source):
        target = wrap(dm + i)
        blocks = GROUP // 2
        return remote(
            dsend.at[part, pl.ds(target * PAIRS + k * blocks, blocks)],
            held[part].at[pl.ds(source * PAIRS + k * blocks, blocks)],
            d_send.at[part * GROUPS + k, i], d_recv.at[part * GROUPS + k, source], (target, vm),
        )

    def slab_copy(i, source):
        return remote(slab, table.at[source], slab_send.at[i], slab_recv.at[source],
                      (wrap(dm + i), vm))

    def send_bands(part, k):
        others(lambda i: band_copy(part, k, i, dm).start())
        for j in range(GROUP // 2):
            block = dm * PAIRS + k * (GROUP // 2) + j
            held[part][block] = dsend[part, block]

    def wait_bands(part):
        for k in range(GROUPS):
            others(lambda i: band_copy(part, k, i, wrap(dm + i)).wait_recv())

    half = CAP // 2

    def other_chip(n):
        return lax.rem(chip + n, CHIPS)

    def tile_copy(part, n, source):
        sender = 2 * source + core
        target = other_chip(n)
        return remote(
            zsend.at[part, pl.ds(target * half, half)], zrecv[part].at[pl.ds(sender * half, half)],
            z_send.at[part, n], z_recv.at[part, source], (dm, 2 * target + core),
        )

    def pass_copy(part, source, source_core):
        block = pl.ds((2 * source + source_core) * half, half)
        return remote(
            zrecv[part].at[block], zrecv[part].at[block],
            pass_send.at[part, source], pass_recv.at[part, source], (dm, 2 * chip + 1 - core),
        )

    first_rows = sub8 < 4

    def two_pieces(part, target, j):
        a = sidx[target, 2 * j]
        b = sidx[target, 2 * j + 1]
        x = held[part][a >> 1]
        y = held[part][b >> 1]
        x = jnp.where((a & 1) == 1, pltpu.roll(x, 4, 0), x)
        y = jnp.where((b & 1) == 1, y, pltpu.roll(y, 4, 0))
        return jnp.where(first_rows, x, y)

    def send_tiles(part):
        def pack(n, carry):
            target = other_chip(n)
            for j in range(half):
                zsend[part, target * half + j] = two_pieces(part, 2 * target, j)
            tile_copy(part, n, chip).start()
            return carry

        lax.fori_loop(1, CHIPS, pack, 0)
        for j in range(half):
            zrecv[part][vm * half + j] = two_pieces(part, 2 * chip, j)
        pass_copy(part, chip, core).start()

    def list_tiles():
        others(lambda i: slab_copy(i, wrap(dm + i)).wait_recv())
        listed = jnp.zeros((N, 128), jnp.int32)
        count = jnp.zeros((N, 128), jnp.int32)
        for d in range(N):
            slot = jnp.max(jnp.where(table[d] == vm, lane16, -1), axis=1, keepdims=True)
            wanted = slot >= 0
            hits = jnp.broadcast_to(jnp.where(wanted, 1, 0), (N, 128))
            beside = partner_row(hits)
            rank = count + jnp.where(second, beside, 0)
            listed = listed + jnp.where(wanted & (lane16 == rank), slot + d * SLOTS, 0)
            count = count + hits + beside
        listed = listed + partner_row(listed)
        vidx[...] = listed
        index_copy().start()

    def index_copy():
        return pltpu.make_async_copy(vidx, sidx, local_sem.at[0])

    def early(t, carry):
        render_one(0, t)

        @pl.when(t == 3)
        def _():
            pl.semaphore_wait(barrier, 2 * (N - 1) + 4)
            others(lambda i: row_copy(i, vm).start())

        for k in range(GROUPS):
            @pl.when(t == (k + 1) * GROUP - 1)
            def _(k=k):
                send_bands(0, k)

        return carry

    lax.fori_loop(0, SLOTS, early, 0)

    def late(t, carry):
        render_one(1, t)

        @pl.when(t == 0)
        def _():
            others(lambda i: row_copy(i, wrap(vm + i)).wait_recv())
            for v in range(N):
                slab[pl.ds(v, 1), :] = row_in[v, pl.ds(0, 1), :]
            table[dm] = slab[...]
            others(lambda i: slab_copy(i, dm).start())

        for k in range(GROUPS):
            @pl.when(t == (k + 1) * GROUP - 1)
            def _(k=k):
                send_bands(1, k)

        @pl.when(t == 5)
        def _():
            list_tiles()

        @pl.when(t == 6)
        def _():
            index_copy().wait()
            wait_bands(0)
            send_tiles(0)

        return carry

    lax.fori_loop(0, SLOTS, late, 0)
    wait_bands(1)
    send_tiles(1)

    count = jnp.zeros((N, 128), jnp.int32)
    for d in range(N):
        named = sub16 == table[d, pl.ds(vm, 1), :]
        pair = [
            jnp.max(jnp.where(sub16 == table[d, pl.ds(2 * chip + c, 1), :], 1, 0), axis=1, keepdims=True)
            for c in range(2)
        ]
        rank = jnp.minimum(count + core * pair[0], CAP - 1)
        place = jnp.where(named, sub16 * CAP + rank + 1, 0)
        vpos[pl.ds(d, 1), :] = jnp.sum(place, axis=0, keepdims=True) - 1
        count = count + pair[0] + pair[1]
    place_copy = pltpu.make_async_copy(vpos, spos, local_sem.at[1])
    place_copy.start()
    place_copy.wait()

    longest = jnp.zeros((N, 128), jnp.int32)
    for h in range(N):
        hits = jnp.zeros((N, 128), jnp.int32)
        for d in range(N):
            hits = hits + jnp.where(table[d] == h, 1, 0)
        each = jnp.broadcast_to(jnp.sum(hits, axis=1, keepdims=True), (N, 128))
        longest = jnp.maximum(longest, each + partner_row(each))
    most[...] = jnp.broadcast_to(jnp.max(longest, axis=0, keepdims=True), (8, 128))

    def compose(part):
        for n in (1, 7, 2, 6, 3, 5, 4):
            tile_copy(part, n, other_chip(n)).wait_recv()
            pass_copy(part, other_chip(n), core).start()
        for n in range(CHIPS):
            pass_copy(part, n, 1 - core).wait_recv()

        def gather(d, carry):
            for t in range(SLOTS):
                place = spos[d, t]
                safe = jnp.maximum(place, 0)
                piece = zrecv[part][safe >> 1]
                piece = jnp.where((safe & 1) == 1, pltpu.roll(piece, 4, 0), piece)
                piece = jnp.where(place >= 0, piece, jnp.zeros_like(piece))
                comp[d, pl.ds(t, 4, stride=8), :] = piece[0:4]
            return carry

        lax.fori_loop(0, N, gather, 0)
        through = jnp.ones((8, 128), jnp.float32)
        sums = [jnp.zeros((8, 128), jnp.float32)] * 4
        for d in range(N):
            layer = [comp[d, pl.ds(ch * 8, 8), :] for ch in range(4)]
            sums = [sums[ch] + through * layer[ch] for ch in range(4)]
            through = through * (1.0 - layer[3])
        return sums

    total = compose(0) + compose(1)
    for r in range(8):
        front[pl.ds(r * 8, 8), :] = total[r]
    edges[0] = front[pl.ds(0, 8, stride=8), :]
    edges[1] = front[pl.ds(7, 8, stride=8), :]

    rim = []
    for n, (dd, dv) in enumerate(SIDES):
        if dv == 0 and dd == -1:
            src, dst = front.at[pl.ds(0, 32), :], below
        elif dv == 0:
            src, dst = front.at[pl.ds(32, 32), :], above
        elif dv == 1:
            src, dst = edges.at[1], from_left.at[1 - dd]
        else:
            src, dst = edges.at[0], from_right.at[1 - dd]
        target = (wrap(dm + dd), wrap(vm + dv))
        rim.append(remote(src, dst, rim_send.at[n], rim_recv.at[n], target))
    for copy in rim:
        copy.start()
    for copy in rim:
        copy.wait_recv()

    low = lane8 < 64
    x = lax.rem(lane8, 64)
    upper = sub8 < 4
    nothing = jnp.zeros((8, 128), jnp.float32)

    def mix(before, mid, after):
        return 0.25 * before + 0.5 * mid + 0.25 * after

    def rows_blurred(before, mid, after):
        up = pltpu.roll(jnp.where(low, mid, before), 64, 1)
        down = pltpu.roll(jnp.where(low, after, mid), 64, 1)
        return mix(up, mid, down)

    def edge_blurred(ref, exists):
        top = jnp.where(dm > 0, ref[0], nothing)
        mid = ref[1]
        bottom = jnp.where(dm < N - 1, ref[2], nothing)
        before = pltpu.roll(jnp.where(upper, mid, top), 4, 0)
        after = pltpu.roll(jnp.where(upper, bottom, mid), 4, 0)
        return jnp.where(exists, rows_blurred(before, mid, after), nothing)

    for copy in rim:
        copy.wait_send()
    side[0] = pltpu.roll(edge_blurred(from_left, vm > 0), 65, 1)
    side[1] = pltpu.roll(edge_blurred(from_right, vm < N - 1), 63, 1)
    for r in range(8):
        ch = r % 4
        if r < 4:
            before = jnp.where(dm > 0, above[pl.ds(ch * 8, 8), :], nothing)
            after = total[4 + ch]
        else:
            before = total[ch]
            after = jnp.where(dm < N - 1, below[pl.ds(ch * 8, 8), :], nothing)
        rows = rows_blurred(before, total[r], after)
        left_in = jnp.broadcast_to(side[0, pl.ds(r, 1), :], (8, 128))
        right_in = jnp.broadcast_to(side[1, pl.ds(r, 1), :], (8, 128))
        over_left = jnp.where(sub8 == 0, left_in, pltpu.roll(pltpu.roll(rows, 65, 1), 1, 0))
        over_right = jnp.where(sub8 == 7, right_in, pltpu.roll(pltpu.roll(rows, 63, 1), 7, 0))
        left = jnp.where(x == 0, over_left, pltpu.roll(rows, 1, 1))
        right = jnp.where(x == 63, over_right, pltpu.roll(rows, 127, 1))
        blurred = mix(left, rows, right)
        front[pl.ds(r * 8, 8), :] = total[r] + SHARPEN * (total[r] - blurred)
    for r in range(8):
        pj, ch = divmod(r, 4)
        even = front[pl.ds(r * 8, 4, stride=2), :]
        odd = front[pl.ds(r * 8 + 1, 4, stride=2), :]
        row0 = jnp.where(low[0:4], even, pltpu.roll(odd, 64, 1))
        row1 = jnp.where(low[0:4], pltpu.roll(even, 64, 1), odd)
        for m in range(4):
            image[ch, pl.ds(2 * pj, 1), pl.ds(m * 128, 128)] = row0[m:m + 1]
            image[ch, pl.ds(2 * pj + 1, 1), pl.ds(m * 128, 128)] = row1[m:m + 1]

    others(lambda i: row_copy(i, vm).wait_send())
    others(lambda i: slab_copy(i, dm).wait_send())
    for part in range(2):
        for n in range(CHIPS):
            if n > 0:
                tile_copy(part, n, chip).wait_send()
            pass_copy(part, n, core).wait_send()
        for k in range(GROUPS):
            others(lambda i: band_copy(part, k, i, dm).wait_send())


def fused(tiles, holders):
    f32, i32 = jnp.float32, jnp.int32
    dma = pltpu.SemaphoreType.DMA
    return pl.pallas_call(
        fused_kernel,
        in_specs=[
            pl.BlockSpec(memory_space=pl.ANY),
            pl.BlockSpec(memory_space=pl.ANY),
        ],
        out_specs=(pl.BlockSpec(memory_space=pltpu.VMEM), pl.BlockSpec(memory_space=pltpu.VMEM)),
        out_shape=(jax.ShapeDtypeStruct((4, 4, SLOTS * 64), f32), jax.ShapeDtypeStruct((8, 128), i32)),
        scratch_shapes=[
            pltpu.SMEM((1, SLOTS), i32),
            pltpu.VMEM((SLOTS, 4, 8, 8, 8, 128), f32),
            pltpu.VMEM((2, N * PAIRS, 8, 128), f32),
            pltpu.VMEM((N * PAIRS, 8, 128), f32),
            pltpu.VMEM((N * PAIRS, 8, 128), f32),
            pltpu.VMEM((2, CHIPS * CAP // 2, 8, 128), f32),
            pltpu.VMEM((N * CAP // 2, 8, 128), f32),
            pltpu.VMEM((N * CAP // 2, 8, 128), f32),
            pltpu.VMEM((N, 32, 128), f32),
            pltpu.VMEM((N, 8, 128), i32),
            pltpu.VMEM((N, 128), i32),
            pltpu.VMEM((N, N, 128), i32),
            pltpu.VMEM((N, 128), i32),
            pltpu.VMEM((N, 128), i32),
            pltpu.SMEM((N, 128), i32),
            pltpu.SMEM((N, 128), i32),
            pltpu.VMEM((64, 128), f32),
            pltpu.VMEM((2, 8, 128), f32),
            pltpu.VMEM((32, 128), f32),
            pltpu.VMEM((32, 128), f32),
            pltpu.VMEM((3, 8, 128), f32),
            pltpu.VMEM((3, 8, 128), f32),
            pltpu.VMEM((2, 8, 128), f32),
            dma((2, CHIPS)), dma((2, CHIPS)),
            dma((SLOTS, 4)), dma((N,)), dma((N,)), dma((N,)), dma((N,)), dma((3,)),
            dma((2 * GROUPS, N)), dma((2 * GROUPS, N)), dma((2, CHIPS)), dma((2, CHIPS)), dma((8,)), dma((8,)),
        ],
        compiler_params=pltpu.CompilerParams(
            collective_id=0, has_side_effects=True, vmem_limit_bytes=58 * 1024 * 1024
        ),
        name="fused",
    )(holders, tiles)


def render_kernel(bricks_ref, out_ref):
    def load(z, g):
        return bricks_ref[0, z // 8, pl.ds(g * 8 + z % 8, 8, stride=32), :]

    def store(ch, g, value):
        out_ref[0, pl.ds((g // 2) * 8 + ch * 2 + g % 2, 8, stride=16), :] = value

    render_slot(load, store)


def render(bricks):
    slots = bricks.shape[0]
    return pl.pallas_call(
        render_kernel,
        grid=(slots,),
        in_specs=[pl.BlockSpec((1, 8, 256, 128), lambda t: (t, 0, 0, 0))],
        out_specs=pl.BlockSpec((1, 128, 128), lambda t: (t, 0, 0)),
        out_shape=jax.ShapeDtypeStruct((slots, 128, 128), jnp.float32),
        name="render",
    )(bricks)


def padded_2(x, sides, width):
    for axis, dim in sides:
        size, length = (lax.axis_size(axis), x.shape[dim])
        up = [(i, (i + 1) % size) for i in range(size - 1)]
        down = [(j, i) for i, j in up]
        last = lax.slice_in_dim(x, length - width, length, axis=dim)
        initial = lax.slice_in_dim(x, 0, width, axis=dim)
        before = lax.ppermute(last, axis, up)
        after = lax.ppermute(initial, axis, down)
        x = jnp.concatenate([before, x, after], axis=dim)
    return x


def by_collectives(bricks, tile_holder):
    me = lax.axis_index("view")
    tiles = render(as_tiles(bricks[0, 0]))
    table = lax.all_gather(tile_holder[0, 0], "view")
    table = lax.all_gather(table, "depth")
    slot_ids = jnp.arange(8, dtype=jnp.int32)
    slot = jnp.max(jnp.where(table == me, slot_ids, 0), axis=2)
    bands = tiles.reshape(8, 16, 8, 128).transpose(1, 0, 2, 3)
    held = lax.all_to_all(bands, "depth", split_axis=0, concat_axis=0, tiled=True)
    flat = held.reshape(16 * 8, 8, 128)
    index = (jnp.arange(16, dtype=jnp.int32)[None, :] * 8 + slot.T).reshape(-1)
    outgoing = flat[index].reshape(16, 16, 8, 128)
    arrived = lax.all_to_all(outgoing, "view", split_axis=0, concat_axis=0, tiled=True)
    mine = lax.dynamic_index_in_dim(table, me, 1, keepdims=False)
    where_at = jnp.maximum(mine, 0) * 16 + jnp.arange(16, dtype=jnp.int32)[:, None]
    pieces = arrived.reshape(256, 8, 128)[where_at.reshape(-1)].reshape(16, 8, 4, 2, 128)
    pieces = pieces * (mine >= 0).astype(jnp.float32)[:, :, None, None, None]
    current = pieces
    while current.shape[0] > 1:
        pair = current.reshape((current.shape[0] // 2, 2) + current.shape[1:])
        current = pair[:, 0] + (1.0 - pair[:, 0, :, 3:4]) * pair[:, 1]
    merged = current[0]
    block = merged.reshape(8, 4, 4, 64).transpose(1, 2, 0, 3).reshape(4, 4, 512)
    padded = padded_2(block, (("depth", 1), ("view", 2)), 1)
    rows_done = 0.25 * padded[:, :-2] + 0.5 * padded[:, 1:-1] + 0.25 * padded[:, 2:]
    blurred = 0.25 * rows_done[:, :, :-2] + 0.5 * rows_done[:, :, 1:-1] + 0.25 * rows_done[:, :, 2:]
    return block + SHARPEN * (block - blurred)


def body(bricks, tile_holder):
    tiles = as_tiles(bricks[0, 0]).reshape(SLOTS, 8, 8, 4, 8, 128)
    image, most = fused(tiles, tile_holder[0])
    return lax.cond(
        most[0, 0] > CAP, lambda: by_collectives(bricks, tile_holder), lambda: image
    )


def solution(mesh):
    in_specs = (P("depth", "view", None, None, None), P("depth", "view", None))
    out_specs = P(None, "depth", "view")
    return jax.shard_map(body, mesh=mesh, in_specs=in_specs, out_specs=out_specs, check_vma=False)
```

```python
import math

import jax
import jax.numpy as jnp
from jax import lax
from jax.experimental import pallas as pl
from jax.experimental.pallas import tpu as pltpu
from jax.sharding import PartitionSpec as P

STEPS = 48
DENSITY = 0.8
SHARPEN = 1.5
PERIODS = 16
UNROLL = 4
HALF = DENSITY / STEPS / 2.0
LOG2E = math.log2(math.e)


def render_slot(load, store):
    shape = (8, 128)
    lane = lax.broadcasted_iota(jnp.int32, shape, 1)
    row = lax.broadcasted_iota(jnp.int32, shape, 0)
    x = lax.rem(lane, 64)
    first_x = x == 0
    last_x = x == 63
    low = lane < 64
    top = row == 0
    bottom = row == 7

    def plane_terms(cur):
        out = []
        swapped = [pltpu.roll(c, 64, 1) for c in cur]
        before0 = jnp.where(top, cur[0], pltpu.roll(swapped[3], 1, 0))
        delta = [swapped[0] - before0]
        for g in range(1, 4):
            delta.append(swapped[g] - swapped[g - 1])
        delta.append(jnp.where(bottom, cur[3] - swapped[3], pltpu.roll(delta[0], 7, 0)))
        for g in range(4):
            c = cur[g]
            right = jnp.where(last_x, c, pltpu.roll(c, 127, 1))
            left = jnp.where(first_x, c, pltpu.roll(c, 1, 1))
            gx = right - left
            gy = jnp.where(low, delta[g], delta[g + 1])
            out.append(gx * gx + gy * gy + 36.0)
        return out

    def shade_step(state, cur, plane, behind, ahead):
        trans, acc_a, acc_b, acc_c = state
        new = ([], [], [], [])
        for g in range(4):
            c = cur[g]
            gz = ahead[g] - behind[g]
            slope = jnp.abs(gz) * lax.rsqrt(plane[g] + gz * gz)
            dense = jnp.tanh(c * (1.0 / 3.0) - 2.0)
            kept = jnp.exp2(dense * (-LOG2E * HALF) + (-LOG2E * HALF))
            after = trans[g] * kept
            lit = (trans[g] - after) * (slope + (3.0 / 7.0))
            new[0].append(after)
            new[1].append(acc_a[g] + lit)
            new[2].append(acc_b[g] + lit * jnp.tanh(c * 0.125))
            new[3].append(acc_c[g] + lit * jnp.tanh(c * 0.25 - 1.5))
        return new

    def period_samples(k):
        three = ([], [], [])
        for g in range(4):
            b0, b1, b2, b3 = (load(4 * k + j, g) for j in range(4))
            three[0].append(5.0 * b0 + b1)
            three[1].append(3.0 * (b1 + b2))
            three[2].append(b2 + 5.0 * b3)
        return three

    zeros = [jnp.zeros(shape, jnp.float32)] * 4
    ones = [jnp.ones(shape, jnp.float32)] * 4
    state = (ones, zeros, zeros, zeros)
    p0, p1, p2 = period_samples(0)
    state = shade_step(state, p0, plane_terms(p0), p0, p1)
    state = shade_step(state, p1, plane_terms(p1), p0, p2)
    carry = (p1, p2, plane_terms(p2), state)

    def one_period(k, carry):
        behind, last, last_plane, state = carry
        a, b, c = period_samples(k)
        state = shade_step(state, last, last_plane, behind, a)
        state = shade_step(state, a, plane_terms(a), last, b)
        state = shade_step(state, b, plane_terms(b), a, c)
        return (b, c, plane_terms(c), state)

    carry = lax.fori_loop(1, PERIODS, one_period, carry, unroll=True)
    behind, last, last_plane, state = carry
    trans, acc_a, acc_b, acc_c = shade_step(state, last, last_plane, behind, last)
    for g in range(4):
        store(0, g, 0.35 * (acc_a[g] + acc_b[g]))
        store(1, g, 0.35 * (acc_a[g] - acc_b[g]))
        store(2, g, 0.35 * (acc_a[g] + acc_c[g]))
        store(3, g, 1.0 - trans[g])


def as_tiles(stored):
    slots, edge, pixels = stored.shape
    split = stored.reshape(slots, edge // 8, 8, pixels // 128, 128)
    return split.transpose(0, 1, 3, 2, 4).reshape(slots, edge // 8, pixels // 16, 128)


def render_part(load, store, part):
    shape = (8, 128)
    kept_rows = (part, part + 2)
    lane = lax.broadcasted_iota(jnp.int32, shape, 1)
    row = lax.broadcasted_iota(jnp.int32, shape, 0)
    x = lax.rem(lane, 64)
    first_x = x == 0
    last_x = x == 63
    low = lane < 64
    top = row == 0
    bottom = row == 7

    def plane_terms(cur):
        swapped = [pltpu.roll(c, 64, 1) for c in cur]
        if part == 0:
            delta = [swapped[0] - jnp.where(top, cur[0], pltpu.roll(swapped[3], 1, 0))]
        else:
            delta = [None]
        for g in range(1, 4):
            delta.append(swapped[g] - swapped[g - 1])
        if part == 1:
            delta.append(jnp.where(bottom, cur[3], pltpu.roll(swapped[0], 7, 0)) - swapped[3])
        out = []
        for g in kept_rows:
            c = cur[g]
            right = jnp.where(last_x, c, pltpu.roll(c, 127, 1))
            left = jnp.where(first_x, c, pltpu.roll(c, 1, 1))
            gx = right - left
            gy = jnp.where(low, delta[g], delta[g + 1])
            out.append(gx * gx + gy * gy + 36.0)
        return out

    def shade_step(state, cur, plane, behind, ahead):
        trans, acc_a, acc_b, acc_c = state
        new = ([], [], [], [])
        for n, g in enumerate(kept_rows):
            c = cur[g]
            gz = ahead[g] - behind[g]
            slope = jnp.abs(gz) * lax.rsqrt(plane[n] + gz * gz)
            dense = jnp.tanh(c * (1.0 / 3.0) - 2.0)
            kept = jnp.exp2(dense * (-LOG2E * HALF) + (-LOG2E * HALF))
            after = trans[n] * kept
            lit = (trans[n] - after) * (slope + (3.0 / 7.0))
            new[0].append(after)
            new[1].append(acc_a[n] + lit)
            new[2].append(acc_b[n] + lit * jnp.tanh(c * 0.125))
            new[3].append(acc_c[n] + lit * jnp.tanh(c * 0.25 - 1.5))
        return new

    def period_samples(k):
        three = ([], [], [])
        for g in range(4):
            b0, b1, b2, b3 = (load(4 * k + j, g) for j in range(4))
            three[0].append(5.0 * b0 + b1)
            three[1].append(3.0 * (b1 + b2))
            three[2].append(b2 + 5.0 * b3)
        return three

    zeros = [jnp.zeros(shape, jnp.float32)] * 2
    ones = [jnp.ones(shape, jnp.float32)] * 2
    state = (ones, zeros, zeros, zeros)
    p0, p1, p2 = period_samples(0)
    state = shade_step(state, p0, plane_terms(p0), p0, p1)
    state = shade_step(state, p1, plane_terms(p1), p0, p2)
    carry = (p1, p2, plane_terms(p2), state)

    def one_period(k, carry):
        behind, last, last_plane, state = carry
        a, b, c = period_samples(k)
        state = shade_step(state, last, last_plane, behind, a)
        state = shade_step(state, a, plane_terms(a), last, b)
        state = shade_step(state, b, plane_terms(b), a, c)
        return (b, c, plane_terms(c), state)

    carry = lax.fori_loop(1, PERIODS, one_period, carry, unroll=True)
    behind, last, last_plane, state = carry
    trans, acc_a, acc_b, acc_c = shade_step(state, last, last_plane, behind, last)
    for n, g in enumerate(kept_rows):
        store(0, g, 0.35 * (acc_a[n] + acc_b[n]))
        store(1, g, 0.35 * (acc_a[n] - acc_b[n]))
        store(2, g, 0.35 * (acc_a[n] + acc_c[n]))
        store(3, g, 1.0 - trans[n])


N = 16
SLOTS = 8
PAIRS = SLOTS // 2
GROUPS = 2
GROUP = SLOTS // GROUPS
CHIPS = N // 2
CAP = 20
MESH = pl.DeviceIdType.MESH
SIDES = [(dd, dv) for dd in (-1, 0, 1) for dv in (-1, 0, 1) if (dd, dv) != (0, 0)]


def wrap(i):
    return lax.rem(i + N, N)


def fused_kernel(
    holders, bricks, image, most, names, buf, dsend, held0, held1, zsend, zrecv0, zrecv1, comp, row_in, slab, table,
    vidx, vpos, sidx, spos, front, edges, above, below, from_left, from_right, side,
    pass_send, pass_recv, brick_sem, row_send, row_recv, slab_send, slab_recv, local_sem,
    d_send, d_recv, z_send, z_recv, rim_send, rim_recv,
):
    dm = lax.axis_index("depth")
    vm = lax.axis_index("view")
    held = (held0, held1)
    chip = vm // 2
    core = lax.rem(vm, 2)
    zrecv = (zrecv0, zrecv1)
    lane8 = lax.broadcasted_iota(jnp.int32, (8, 128), 1)
    sub8 = lax.broadcasted_iota(jnp.int32, (8, 128), 0)
    lane16 = lax.broadcasted_iota(jnp.int32, (N, 128), 1)
    sub16 = lax.broadcasted_iota(jnp.int32, (N, 128), 0)
    second = lax.rem(sub16, 2) == 1

    def partner_row(x):
        return jnp.where(second, pltpu.roll(x, 1, 0), pltpu.roll(x, N - 1, 0))

    def remote(src, dst, send, recv, target):
        return pltpu.make_async_remote_copy(
            src_ref=src, dst_ref=dst, send_sem=send, recv_sem=recv,
            device_id=target, device_id_type=MESH,
        )

    def others(step):
        def run(i, carry):
            step(i)
            return carry
        lax.fori_loop(1, N, run, 0)

    barrier = pltpu.get_barrier_semaphore()

    def greet(i):
        pl.semaphore_signal(barrier, inc=1, device_id=(dm, wrap(vm + i)), device_id_type=MESH)
        pl.semaphore_signal(barrier, inc=1, device_id=(wrap(dm + i), vm), device_id_type=MESH)

    others(greet)
    for dd, dv in SIDES:
        if dd != 0 and dv != 0:
            target = (wrap(dm + dd), wrap(vm + dv))
            pl.semaphore_signal(barrier, inc=1, device_id=target, device_id_type=MESH)

    def brick_copy(t, g):
        return pltpu.make_async_copy(bricks.at[t, :, :, g], buf.at[t, g], brick_sem.at[t, g])

    for t in range(SLOTS):
        for g in range(4):
            brick_copy(t, g).start()
    holder_copy = pltpu.make_async_copy(holders, names, local_sem.at[2])
    holder_copy.start()

    holder_copy.wait()
    mine = jnp.full((8, 128), -1, jnp.int32)
    for t in range(SLOTS):
        mine = jnp.where(lane8 == t, names[0, t], mine)
    row_in[vm] = mine

    def row_copy(i, source):
        return remote(row_in.at[source], row_in.at[source], row_send.at[i], row_recv.at[source],
                      (dm, wrap(vm + i)))

    def render_one(part, t):
        if part == 0:
            for g in range(4):
                brick_copy(t, g).wait()
        voxels = buf.reshape(SLOTS * 4 * 8 * 64, 128)

        def load(z, g):
            first = ((t * 4 + g) * 8 + z // 8) * 64 + z % 8
            return voxels[pl.ds(first, 8, stride=8), :]

        flat = dsend.reshape(2 * N * PAIRS * 8, 128)

        def store(ch, g, value):
            first = part * N * SLOTS * 4 + ((g // 2) * SLOTS + t) * 4 + ch
            flat[pl.ds(first, 8, stride=2 * SLOTS * 4), :] = value

        render_part(load, store, part)

    def band_copy(part, k, i, source):
        target = wrap(dm + i)
        blocks = GROUP // 2
        return remote(
            dsend.at[part, pl.ds(target * PAIRS + k * blocks, blocks)],
            held[part].at[pl.ds(source * PAIRS + k * blocks, blocks)],
            d_send.at[part * GROUPS + k, i], d_recv.at[part * GROUPS + k, source], (target, vm),
        )

    def slab_copy(i, source):
        return remote(slab, table.at[source], slab_send.at[i], slab_recv.at[source],
                      (wrap(dm + i), vm))

    def send_bands(part, k):
        others(lambda i: band_copy(part, k, i, dm).start())
        for j in range(GROUP // 2):
            block = dm * PAIRS + k * (GROUP // 2) + j
            held[part][block] = dsend[part, block]

    def wait_bands(part):
        for k in range(GROUPS):
            others(lambda i: band_copy(part, k, i, wrap(dm + i)).wait_recv())

    half = CAP // 2

    def other_chip(n):
        return lax.rem(chip + n, CHIPS)

    def tile_copy(part, n, source):
        sender = 2 * source + core
        target = other_chip(n)
        return remote(
            zsend.at[part, pl.ds(target * half, half)], zrecv[part].at[pl.ds(sender * half, half)],
            z_send.at[part, n], z_recv.at[part, source], (dm, 2 * target + core),
        )

    def pass_copy(part, source, source_core):
        block = pl.ds((2 * source + source_core) * half, half)
        return remote(
            zrecv[part].at[block], zrecv[part].at[block],
            pass_send.at[part, source], pass_recv.at[part, source], (dm, 2 * chip + 1 - core),
        )

    first_rows = sub8 < 4

    def two_pieces(part, target, j):
        a = sidx[target, 2 * j]
        b = sidx[target, 2 * j + 1]
        x = held[part][a >> 1]
        y = held[part][b >> 1]
        x = jnp.where((a & 1) == 1, pltpu.roll(x, 4, 0), x)
        y = jnp.where((b & 1) == 1, y, pltpu.roll(y, 4, 0))
        return jnp.where(first_rows, x, y)

    def send_tiles(part):
        def pack(n, carry):
            target = other_chip(n)
            for j in range(half):
                zsend[part, target * half + j] = two_pieces(part, 2 * target, j)
            tile_copy(part, n, chip).start()
            return carry

        lax.fori_loop(1, CHIPS, pack, 0)
        for j in range(half):
            zrecv[part][vm * half + j] = two_pieces(part, 2 * chip, j)
        pass_copy(part, chip, core).start()

    def list_tiles():
        others(lambda i: slab_copy(i, wrap(dm + i)).wait_recv())
        listed = jnp.zeros((N, 128), jnp.int32)
        count = jnp.zeros((N, 128), jnp.int32)
        for d in range(N):
            slot = jnp.max(jnp.where(table[d] == vm, lane16, -1), axis=1, keepdims=True)
            wanted = slot >= 0
            hits = jnp.broadcast_to(jnp.where(wanted, 1, 0), (N, 128))
            beside = partner_row(hits)
            rank = count + jnp.where(second, beside, 0)
            listed = listed + jnp.where(wanted & (lane16 == rank), slot + d * SLOTS, 0)
            count = count + hits + beside
        listed = listed + partner_row(listed)
        vidx[...] = listed
        index_copy().start()

    def index_copy():
        return pltpu.make_async_copy(vidx, sidx, local_sem.at[0])

    def early(t, carry):
        render_one(0, t)

        @pl.when(t == 3)
        def _():
            pl.semaphore_wait(barrier, 2 * (N - 1) + 4)
            others(lambda i: row_copy(i, vm).start())

        for k in range(GROUPS):
            @pl.when(t == (k + 1) * GROUP - 1)
            def _(k=k):
                send_bands(0, k)

        return carry

    lax.fori_loop(0, SLOTS, early, 0)

    def late(t, carry):
        render_one(1, t)

        @pl.when(t == 0)
        def _():
            others(lambda i: row_copy(i, wrap(vm + i)).wait_recv())
            for v in range(N):
                slab[pl.ds(v, 1), :] = row_in[v, pl.ds(0, 1), :]
            table[dm] = slab[...]
            others(lambda i: slab_copy(i, dm).start())

        for k in range(GROUPS):
            @pl.when(t == (k + 1) * GROUP - 1)
            def _(k=k):
                send_bands(1, k)

        @pl.when(t == 5)
        def _():
            list_tiles()

        @pl.when(t == 6)
        def _():
            index_copy().wait()
            wait_bands(0)
            send_tiles(0)

        return carry

    lax.fori_loop(0, SLOTS, late, 0)
    wait_bands(1)
    send_tiles(1)

    count = jnp.zeros((N, 128), jnp.int32)
    for d in range(N):
        named = sub16 == table[d, pl.ds(vm, 1), :]
        pair = [
            jnp.max(jnp.where(sub16 == table[d, pl.ds(2 * chip + c, 1), :], 1, 0), axis=1, keepdims=True)
            for c in range(2)
        ]
        rank = jnp.minimum(count + core * pair[0], CAP - 1)
        place = jnp.where(named, sub16 * CAP + rank + 1, 0)
        vpos[pl.ds(d, 1), :] = jnp.sum(place, axis=0, keepdims=True) - 1
        count = count + pair[0] + pair[1]
    place_copy = pltpu.make_async_copy(vpos, spos, local_sem.at[1])
    place_copy.start()
    place_copy.wait()

    longest = jnp.zeros((N, 128), jnp.int32)
    for h in range(N):
        hits = jnp.zeros((N, 128), jnp.int32)
        for d in range(N):
            hits = hits + jnp.where(table[d] == h, 1, 0)
        each = jnp.broadcast_to(jnp.sum(hits, axis=1, keepdims=True), (N, 128))
        longest = jnp.maximum(longest, each + partner_row(each))
    most[0, 0] = jnp.max(longest)

    def compose(part):
        for n in (4, 3, 5, 2, 6, 1, 7):
            tile_copy(part, n, other_chip(n)).wait_recv()
            pass_copy(part, other_chip(n), core).start()
        for n in range(CHIPS):
            pass_copy(part, n, 1 - core).wait_recv()

        def gather(d, carry):
            for t in range(SLOTS):
                place = spos[d, t]
                safe = jnp.maximum(place, 0)
                piece = zrecv[part][safe >> 1]
                piece = jnp.where((safe & 1) == 1, pltpu.roll(piece, 4, 0), piece)
                piece = jnp.where(place >= 0, piece, jnp.zeros_like(piece))
                comp[d, pl.ds(t, 4, stride=8), :] = piece[0:4]
            return carry

        lax.fori_loop(0, N, gather, 0)
        through = jnp.ones((8, 128), jnp.float32)
        sums = [jnp.zeros((8, 128), jnp.float32)] * 4
        for d in range(N):
            layer = [comp[d, pl.ds(ch * 8, 8), :] for ch in range(4)]
            sums = [sums[ch] + through * layer[ch] for ch in range(4)]
            through = through * (1.0 - layer[3])
        return sums

    total = compose(0) + compose(1)
    for r in range(8):
        front[pl.ds(r * 8, 8), :] = total[r]
    edges[0] = front[pl.ds(0, 8, stride=8), :]
    edges[1] = front[pl.ds(7, 8, stride=8), :]

    rim = []
    for n, (dd, dv) in enumerate(SIDES):
        if dv == 0 and dd == -1:
            src, dst = front.at[pl.ds(0, 32), :], below
        elif dv == 0:
            src, dst = front.at[pl.ds(32, 32), :], above
        elif dv == 1:
            src, dst = edges.at[1], from_left.at[1 - dd]
        else:
            src, dst = edges.at[0], from_right.at[1 - dd]
        target = (wrap(dm + dd), wrap(vm + dv))
        rim.append(remote(src, dst, rim_send.at[n], rim_recv.at[n], target))
    for copy in rim:
        copy.start()
    for copy in rim:
        copy.wait_recv()

    low = lane8 < 64
    x = lax.rem(lane8, 64)
    upper = sub8 < 4
    nothing = jnp.zeros((8, 128), jnp.float32)

    def mix(before, mid, after):
        return 0.25 * before + 0.5 * mid + 0.25 * after

    def rows_blurred(before, mid, after):
        up = pltpu.roll(jnp.where(low, mid, before), 64, 1)
        down = pltpu.roll(jnp.where(low, after, mid), 64, 1)
        return mix(up, mid, down)

    def edge_blurred(ref, exists):
        top = jnp.where(dm > 0, ref[0], nothing)
        mid = ref[1]
        bottom = jnp.where(dm < N - 1, ref[2], nothing)
        before = pltpu.roll(jnp.where(upper, mid, top), 4, 0)
        after = pltpu.roll(jnp.where(upper, bottom, mid), 4, 0)
        return jnp.where(exists, rows_blurred(before, mid, after), nothing)

    for copy in rim:
        copy.wait_send()
    side[0] = pltpu.roll(edge_blurred(from_left, vm > 0), 65, 1)
    side[1] = pltpu.roll(edge_blurred(from_right, vm < N - 1), 63, 1)
    for r in range(8):
        ch = r % 4
        if r < 4:
            before = jnp.where(dm > 0, above[pl.ds(ch * 8, 8), :], nothing)
            after = total[4 + ch]
        else:
            before = total[ch]
            after = jnp.where(dm < N - 1, below[pl.ds(ch * 8, 8), :], nothing)
        rows = rows_blurred(before, total[r], after)
        left_in = jnp.broadcast_to(side[0, pl.ds(r, 1), :], (8, 128))
        right_in = jnp.broadcast_to(side[1, pl.ds(r, 1), :], (8, 128))
        over_left = jnp.where(sub8 == 0, left_in, pltpu.roll(pltpu.roll(rows, 65, 1), 1, 0))
        over_right = jnp.where(sub8 == 7, right_in, pltpu.roll(pltpu.roll(rows, 63, 1), 7, 0))
        left = jnp.where(x == 0, over_left, pltpu.roll(rows, 1, 1))
        right = jnp.where(x == 63, over_right, pltpu.roll(rows, 127, 1))
        blurred = mix(left, rows, right)
        front[pl.ds(r * 8, 8), :] = total[r] + SHARPEN * (total[r] - blurred)
    for r in range(8):
        pj, ch = divmod(r, 4)
        even = front[pl.ds(r * 8, 4, stride=2), :]
        odd = front[pl.ds(r * 8 + 1, 4, stride=2), :]
        row0 = jnp.where(low[0:4], even, pltpu.roll(odd, 64, 1))
        row1 = jnp.where(low[0:4], pltpu.roll(even, 64, 1), odd)
        for m in range(4):
            image[ch, pl.ds(2 * pj, 1), pl.ds(m * 128, 128)] = row0[m:m + 1]
            image[ch, pl.ds(2 * pj + 1, 1), pl.ds(m * 128, 128)] = row1[m:m + 1]

    others(lambda i: row_copy(i, vm).wait_send())
    others(lambda i: slab_copy(i, dm).wait_send())
    for part in range(2):
        for n in range(CHIPS):
            if n > 0:
                tile_copy(part, n, chip).wait_send()
            pass_copy(part, n, core).wait_send()
        for k in range(GROUPS):
            others(lambda i: band_copy(part, k, i, dm).wait_send())


def fused(tiles, holders):
    f32, i32 = jnp.float32, jnp.int32
    dma = pltpu.SemaphoreType.DMA
    return pl.pallas_call(
        fused_kernel,
        in_specs=[
            pl.BlockSpec(memory_space=pl.ANY),
            pl.BlockSpec(memory_space=pl.ANY),
        ],
        out_specs=(pl.BlockSpec(memory_space=pltpu.VMEM), pl.BlockSpec(memory_space=pltpu.SMEM)),
        out_shape=(jax.ShapeDtypeStruct((4, 4, SLOTS * 64), f32), jax.ShapeDtypeStruct((1, 1), i32)),
        scratch_shapes=[
            pltpu.SMEM((1, SLOTS), i32),
            pltpu.VMEM((SLOTS, 4, 8, 8, 8, 128), f32),
            pltpu.VMEM((2, N * PAIRS, 8, 128), f32),
            pltpu.VMEM((N * PAIRS, 8, 128), f32),
            pltpu.VMEM((N * PAIRS, 8, 128), f32),
            pltpu.VMEM((2, CHIPS * CAP // 2, 8, 128), f32),
            pltpu.VMEM((N * CAP // 2, 8, 128), f32),
            pltpu.VMEM((N * CAP // 2, 8, 128), f32),
            pltpu.VMEM((N, 32, 128), f32),
            pltpu.VMEM((N, 8, 128), i32),
            pltpu.VMEM((N, 128), i32),
            pltpu.VMEM((N, N, 128), i32),
            pltpu.VMEM((N, 128), i32),
            pltpu.VMEM((N, 128), i32),
            pltpu.SMEM((N, 128), i32),
            pltpu.SMEM((N, 128), i32),
            pltpu.VMEM((64, 128), f32),
            pltpu.VMEM((2, 8, 128), f32),
            pltpu.VMEM((32, 128), f32),
            pltpu.VMEM((32, 128), f32),
            pltpu.VMEM((3, 8, 128), f32),
            pltpu.VMEM((3, 8, 128), f32),
            pltpu.VMEM((2, 8, 128), f32),
            dma((2, CHIPS)), dma((2, CHIPS)),
            dma((SLOTS, 4)), dma((N,)), dma((N,)), dma((N,)), dma((N,)), dma((3,)),
            dma((2 * GROUPS, N)), dma((2 * GROUPS, N)), dma((2, CHIPS)), dma((2, CHIPS)), dma((8,)), dma((8,)),
        ],
        compiler_params=pltpu.CompilerParams(
            collective_id=0, has_side_effects=True, vmem_limit_bytes=58 * 1024 * 1024
        ),
        name="fused",
    )(holders, tiles)


def render_kernel(bricks_ref, out_ref):
    def load(z, g):
        return bricks_ref[0, z // 8, pl.ds(g * 8 + z % 8, 8, stride=32), :]

    def store(ch, g, value):
        out_ref[0, pl.ds((g // 2) * 8 + ch * 2 + g % 2, 8, stride=16), :] = value

    render_slot(load, store)


def render(bricks):
    slots = bricks.shape[0]
    return pl.pallas_call(
        render_kernel,
        grid=(slots,),
        in_specs=[pl.BlockSpec((1, 8, 256, 128), lambda t: (t, 0, 0, 0))],
        out_specs=pl.BlockSpec((1, 128, 128), lambda t: (t, 0, 0)),
        out_shape=jax.ShapeDtypeStruct((slots, 128, 128), jnp.float32),
        name="render",
    )(bricks)


def padded_2(x, sides, width):
    for axis, dim in sides:
        size, length = (lax.axis_size(axis), x.shape[dim])
        up = [(i, (i + 1) % size) for i in range(size - 1)]
        down = [(j, i) for i, j in up]
        last = lax.slice_in_dim(x, length - width, length, axis=dim)
        initial = lax.slice_in_dim(x, 0, width, axis=dim)
        before = lax.ppermute(last, axis, up)
        after = lax.ppermute(initial, axis, down)
        x = jnp.concatenate([before, x, after], axis=dim)
    return x


def by_collectives(bricks, tile_holder):
    me = lax.axis_index("view")
    tiles = render(as_tiles(bricks[0, 0]))
    table = lax.all_gather(tile_holder[0, 0], "view")
    table = lax.all_gather(table, "depth")
    slot_ids = jnp.arange(8, dtype=jnp.int32)
    slot = jnp.max(jnp.where(table == me, slot_ids, 0), axis=2)
    bands = tiles.reshape(8, 16, 8, 128).transpose(1, 0, 2, 3)
    held = lax.all_to_all(bands, "depth", split_axis=0, concat_axis=0, tiled=True)
    flat = held.reshape(16 * 8, 8, 128)
    index = (jnp.arange(16, dtype=jnp.int32)[None, :] * 8 + slot.T).reshape(-1)
    outgoing = flat[index].reshape(16, 16, 8, 128)
    arrived = lax.all_to_all(outgoing, "view", split_axis=0, concat_axis=0, tiled=True)
    mine = lax.dynamic_index_in_dim(table, me, 1, keepdims=False)
    where_at = jnp.maximum(mine, 0) * 16 + jnp.arange(16, dtype=jnp.int32)[:, None]
    pieces = arrived.reshape(256, 8, 128)[where_at.reshape(-1)].reshape(16, 8, 4, 2, 128)
    pieces = pieces * (mine >= 0).astype(jnp.float32)[:, :, None, None, None]
    current = pieces
    while current.shape[0] > 1:
        pair = current.reshape((current.shape[0] // 2, 2) + current.shape[1:])
        current = pair[:, 0] + (1.0 - pair[:, 0, :, 3:4]) * pair[:, 1]
    merged = current[0]
    block = merged.reshape(8, 4, 4, 64).transpose(1, 2, 0, 3).reshape(4, 4, 512)
    padded = padded_2(block, (("depth", 1), ("view", 2)), 1)
    rows_done = 0.25 * padded[:, :-2] + 0.5 * padded[:, 1:-1] + 0.25 * padded[:, 2:]
    blurred = 0.25 * rows_done[:, :, :-2] + 0.5 * rows_done[:, :, 1:-1] + 0.25 * rows_done[:, :, 2:]
    return block + SHARPEN * (block - blurred)


def body(bricks, tile_holder):
    tiles = as_tiles(bricks[0, 0]).reshape(SLOTS, 8, 8, 4, 8, 128)
    image, most = fused(tiles, tile_holder[0])
    return lax.cond(
        most[0, 0] > CAP, lambda: by_collectives(bricks, tile_holder), lambda: image
    )


def solution(mesh):
    in_specs = (P("depth", "view", None, None, None), P("depth", "view", None))
    out_specs = P(None, "depth", "view")
    return jax.shard_map(body, mesh=mesh, in_specs=in_specs, out_specs=out_specs, check_vma=False)
```
